128 devices in a mesh: out: 8 (over x, y_hi), blk: 16 (over y_lo, z, core).
Axes of the slice: x: 4, y: 4 (y_hi: 2, y_lo: 2; y = y_hi * 2 + y_lo), z: 4, core: 2. Of those that a mesh axis runs over, the one named last changes fastest.
Arguments:
- checkpoints: bfloat16 [8, 5, 128, 2048], P('out', None, None, 'blk'), may hold values from -4 to 4
- owner: int32 [8], replicated, may hold values from 0 to 7, each once
- flux_matrix: float32 [5, 5], replicated, may hold values from -2.5 to 2.5
- row_link: int32 [16, 128], P('blk'), may hold values from 0 to 127, each once within a row
- blade_group: int32 [96], replicated, may hold values from 0 to 15
- forcing: float32 [5, 128, 2048], P(None, None, 'blk'), may hold values from -6 to 6
Outputs:
- adjoint: float32 [16, 4, 5, 128, 2048], P('out', None, None, None, 'blk')
- sensitivity: float32 [16, 4], P('out')
The draws below stay inside these ranges and needn't reach their ends.
Inputs may be any that keep to these rules, and one draw needn't show every extreme that they name: Each tile's row_link is a permutation of its rows.
All inputs are finite; a program needn't handle non-finite values.
Results may differ from the reference program's by a relative error of at most 0.0003.
Values may be sent and summed in bfloat16 or wider, within the bound.
A program may use at most 128 MiB of HBM per device.

```python
import math
import jax
import jax.numpy as jnp
from jax import lax

FIELDS = 5
BLADES = 96
AMP = 4
STEPS = 3
R = 128
CW = 128
GROUPS = 16
TILES = 16
NC = 2048
N_OUT = 8


def plant(values, key, smallest, top_value):
    index_at = [jax.random.randint(jax.random.fold_in(key, axis), (), 0, length) for axis, length in enumerate(values.shape)]
    main_axis = values.shape.index(max(values.shape))
    beside = index_at[:main_axis] + [(index_at[main_axis] + 1) % values.shape[main_axis]] + index_at[main_axis + 1:]
    return values.at[tuple(index_at)].set(smallest).at[tuple(beside)].set(top_value)


def block_scale(stream_key, shape, split, low, high):
    factor_of = 1.0
    for dim, parts in split:
        draws = jax.random.uniform(jax.random.fold_in(jax.random.fold_in(stream_key, 6), dim), (parts,), jnp.float32, low / len(split), high / len(split))
        factor_of = factor_of * jnp.repeat(jnp.exp(draws), shape[dim] // parts).reshape((-1,) + (1,) * (len(shape) - 1 - dim))
    return factor_of


def centred(rng, shape, spread, bound, split=(), kind=jnp.bfloat16):
    drawn = spread * jax.random.normal(rng, shape, jnp.float32)
    if split:
        drawn = drawn * block_scale(rng, shape, split, -0.22, 0.18)
    return jnp.clip(drawn, -bound, bound).astype(kind)


def setup_inputs(seed: int = 0) -> dict:
    arg_keys = jax.random.split(jax.random.key(seed), 7)
    return {
        "checkpoints": centred(arg_keys[0], (N_OUT, FIELDS, R, NC), 1.0, 4.0, ((0, 8), (3, 16))),
        "owner": jax.random.permutation(arg_keys[1], N_OUT).astype(jnp.int32),
        "flux_matrix": centred(arg_keys[2], (FIELDS, FIELDS), FIELDS ** -0.5, 2.5, (), jnp.float32),
        "row_link": jax.vmap(lambda own: jax.random.permutation(own, R))(jax.random.split(arg_keys[3], TILES)).reshape((TILES, R)).astype(jnp.int32),
        "blade_group": plant(jax.random.randint(arg_keys[4], (BLADES,), 0, GROUPS), jax.random.fold_in(arg_keys[4], 1), 0, GROUPS - 1).astype(jnp.int32),
        "forcing": centred(arg_keys[5], (FIELDS, R, NC), 1.0, 6.0, ((2, 16),), jnp.float32),
    }


time_step = 0.25
second_diff = 0.1
fourth_diff = 0.02
link_weight = 0.5
two_pi = 2.0 * math.pi

def transposed(mu, state, flux_matrix, inverse):
    plus_one = jnp.roll(mu, -1, axis=-1)
    minus_one = jnp.roll(mu, 1, axis=-1)
    plus_two = jnp.roll(mu, -2, axis=-1)
    minus_two = jnp.roll(mu, 2, axis=-1)
    diff = (minus_one - plus_one) * 0.5
    velocity = state[1]
    flux_part = jnp.einsum('fe,afrc->aerc', flux_matrix, diff, precision=lax.Precision.HIGHEST)
    inner = lax.optimization_barrier(jnp.sum(state[None] * diff, axis=1, keepdims=True))
    is_velocity = (jnp.arange(FIELDS) == 1).astype(jnp.float32)[None, :, None, None]
    jac = flux_part + 0.5 * velocity[None, None] * diff + 0.5 * is_velocity * inner
    lapl = plus_one - 2.0 * mu + minus_one
    quart = plus_two - 4.0 * plus_one + 6.0 * mu - 4.0 * minus_one + minus_two
    tiled = mu.reshape(AMP, FIELDS, R, TILES, CW)
    index = inverse.T.astype(jnp.int32)[None, None, :, :, None]
    linked = jnp.take_along_axis(tiled, index, axis=2).reshape(mu.shape)
    rows_part = mu - linked
    return mu - time_step * (jac - second_diff * lapl + fourth_diff * quart + link_weight * rows_part)

def reference(checkpoints, owner, flux_matrix, row_link, blade_group, forcing):
    total = NC
    column = jnp.arange(total, dtype=jnp.int32)
    scaled = column * BLADES
    blade_of = scaled // total
    phase = (scaled % total).astype(jnp.float32) / total
    group_of = blade_group[blade_of]
    amp_index = jnp.arange(AMP, dtype=jnp.int32)
    order = (amp_index // 2 + 1).astype(jnp.float32)
    angle = two_pi * order[:, None] * phase[None, :]
    harmonic = jnp.where((amp_index % 2 == 0)[:, None], jnp.cos(angle), jnp.sin(angle))
    weight_col = 1.0 + 2.0 * column.astype(jnp.float32) / total
    norm_scale = 1.0 / math.sqrt(FIELDS * R * total)
    inverse = jnp.argsort(row_link, axis=1).astype(jnp.int32)
    states = [checkpoints[owner[step]].astype(jnp.float32) for step in range(STEPS)]
    weighted = forcing * weight_col[None, None, :]

    def one_group(group):
        member = (group_of == group).astype(jnp.float32)
        source_term = forcing[None] * (member[None, :] * harmonic)[:, None, None, :]
        adjoint = jnp.zeros((AMP, FIELDS, R, total), jnp.float32)
        sens = jnp.zeros((AMP,), jnp.float32)
        for step in reversed(range(STEPS)):
            adjoint = transposed(adjoint + source_term, states[step], flux_matrix, inverse)
            sens = sens + lax.optimization_barrier(jnp.sum(adjoint * weighted[None], axis=(1, 2, 3))) * norm_scale
        return (adjoint, sens)
    adjoints, sensitivity = lax.map(one_group, jnp.arange(GROUPS, dtype=jnp.int32))
    return (adjoints, sensitivity)
```

```python
import functools
import math

import jax
import jax.numpy as jnp
import numpy as np
from jax import lax
from jax.experimental import pallas as pl
from jax.experimental.pallas import tpu as pltpu
from jax.sharding import PartitionSpec as P

FIELDS = 5
BLADES = 96
AMP = 4
GRP_DEV = 2
STEPS = 3
R = 128
CW = 128
TILES = 16
NC = TILES * CW
N_OUT = 8
SOL = GRP_DEV * AMP
CH = CW // N_OUT
HB = 16
HF = 8
EXT = CW + 2 * HF

time_step = 0.25
second_diff = 0.1
fourth_diff = 0.02
link_weight = 0.5

UNIT = 1.0 / (time_step * link_weight)
C0 = UNIT * (1.0 - time_step * (2.0 * second_diff + 6.0 * fourth_diff + link_weight))
C1 = UNIT * time_step * (second_diff + 4.0 * fourth_diff)
C2 = -UNIT * time_step * fourth_diff

MESH = pl.DeviceIdType.MESH
F32 = jnp.float32
DIAG = (0, 2, 3, 4)


def harmonics():
    c = np.arange(-HF, CW + HF)
    phase = ((c * BLADES) % NC) / NC
    rows = [
        (np.cos if a % 2 == 0 else np.sin)(2.0 * math.pi * (a // 2 + 1) * phase) for a in range(AMP)
    ]
    table = np.zeros((EXT, 128), np.float32)
    table[:, :AMP] = np.stack(rows, axis=1)
    return table


def kernel(
    owner_s, flux_s, group_hbm, harm_hbm, link_hbm, ckpt_hbm, force_hbm,
    out_hbm, sens_ref,
    ckpt_v, force_v, group_v, harm_v, link_v, slot, picked, chosen, q, f_ext, idx, coef, pat, wf,
    mu_a, mu_b, res, sacc, sall,
    in_sem, p1_s, p1_r, p2_s, p2_r, h_s, h_r, e_s, e_r, s_s, s_r, out_sem,
):
    o = lax.axis_index("out")
    t = lax.axis_index("blk")
    up = lax.rem(t + 1, TILES)
    down = lax.rem(t + TILES - 1, TILES)

    loads = [
        pltpu.make_async_copy(src, dst, in_sem.at[i])
        for i, (src, dst) in enumerate(
            ((ckpt_hbm, ckpt_v), (force_hbm, force_v), (link_hbm, link_v.at[1]), (group_hbm, group_v), (harm_hbm, harm_v))
        )
    ]
    for c in loads:
        c.start()

    barrier = pltpu.get_barrier_semaphore()
    count = 0
    for k in range(1, N_OUT):
        pl.semaphore_signal(barrier, inc=1, device_id=(lax.rem(o + k, N_OUT), t), device_id_type=MESH)
        count += 1
    for side in (up, down):
        for k in range(N_OUT):
            pl.semaphore_signal(barrier, inc=1, device_id=(lax.rem(o + k, N_OUT), side), device_id_type=MESH)
            count += 1
    for k in range(2, TILES - 1):
        pl.semaphore_signal(barrier, inc=1, device_id=(o, lax.rem(t + k, TILES)), device_id_type=MESH)
        count += 1

    def remote(src, dst, send, recv, device):
        return pltpu.make_async_remote_copy(
            src_ref=src, dst_ref=dst, send_sem=send, recv_sem=recv, device_id=device, device_id_type=MESH
        )

    loads[0].wait()
    for f in range(FIELDS):
        slot[f] = ckpt_v[f].astype(F32).T.astype(jnp.bfloat16)
    loads[1].wait()
    for f in range(FIELDS):
        f_ext[f, HF : HF + CW, :] = force_v[f].T
    loads[2].wait()

    pl.semaphore_wait(barrier, count)

    gather = []
    for k in range(1, N_OUT):
        to = lax.rem(o + k, N_OUT)
        gather.append(
            remote(slot.at[:, pl.ds(pl.multiple_of(to * CH, CH), CH), :], picked.at[o], p1_s.at[k], p1_r.at[k], (to, t))
        )
        gather[-1].start()
    edges = [
        remote(f_ext.at[:, pl.ds(CW, HF), :], f_ext.at[:, pl.ds(0, HF), :], e_s.at[0], e_r.at[0], (o, up)),
        remote(f_ext.at[:, pl.ds(HF, HF), :], f_ext.at[:, pl.ds(HF + CW, HF), :], e_s.at[1], e_r.at[1], (o, down)),
        remote(link_v.at[1], link_v.at[0], e_s.at[2], e_r.at[2], (o, up)),
        remote(link_v.at[1], link_v.at[2], e_s.at[3], e_r.at[3], (o, down)),
    ]
    for c in edges:
        c.start()
    mine = pl.ds(pl.multiple_of(o * CH, CH), CH)
    for f in range(FIELDS):
        picked[o, f] = slot[f, mine, :]

    loads[3].wait()
    loads[4].wait()
    lane = lax.broadcasted_iota(jnp.int32, (EXT, 128), 1)
    col = lax.broadcasted_iota(jnp.int32, (EXT, 128), 0) - HF
    column = lax.rem(t * CW + col + NC, NC)
    blade = lax.shift_right_logical(column * BLADES, 11)
    group_of = jnp.sum(jnp.where(blade == lane, jnp.broadcast_to(group_v[...], (EXT, 128)), 0), axis=1, keepdims=True)
    for a in range(AMP):
        wave = harm_v[:, a : a + 1]
        for g in range(GRP_DEV):
            pat[g * AMP + a] = jnp.broadcast_to(jnp.where(group_of == o * GRP_DEV + g, wave, 0.0), (EXT, 128))
    weight = 1.0 + 2.0 * column[HF : HF + CW].astype(F32) / NC
    wf[...] = jnp.zeros_like(wf)
    for f in range(FIELDS):
        wf[f, HF : HF + CW, :] = f_ext[f, HF : HF + CW, :] * weight
    sacc[...] = jnp.zeros_like(sacc)

    for k in range(1, N_OUT):
        gather[k - 1].wait_recv()
    spread = []
    here = pl.ds(pl.multiple_of(HB + o * CH, CH), CH)
    for i, n in enumerate(reversed(range(STEPS))):
        for f in range(FIELDS):
            piece = picked[owner_s[n], f]
            chosen[i, f] = piece
            q[i, f, here, :] = piece
    for i in range(STEPS):
        for k in range(1, N_OUT):
            to = lax.rem(o + k, N_OUT)
            spread.append(remote(chosen.at[i], q.at[i, :, here, :], p2_s.at[i, k], p2_r.at[i, k], (to, t)))
            spread[-1].start()

        @pl.when(o == 0)
        def _():
            for k in range(N_OUT):
                remote(chosen.at[i], q.at[i, :, pl.ds(HB + CW, HB), :], h_s.at[i, k], h_r.at[i, 1], (k, down)).start()

        @pl.when(o == N_OUT - 1)
        def _():
            for k in range(N_OUT):
                remote(chosen.at[i], q.at[i, :, pl.ds(0, HB), :], h_s.at[i, k], h_r.at[i, 0], (k, up)).start()

    for c in edges:
        c.wait_recv()
    sub = lax.broadcasted_iota(jnp.int32, (R, 128), 0)
    lan = lax.broadcasted_iota(jnp.int32, (R, 128), 1)
    for side, (lo, n) in enumerate(((0, HF), (HF, CW), (HF + CW, HF))):
        links = jnp.broadcast_to(link_v[side], (R, 128)).T
        inverse = jnp.sum(jnp.where(links == lan, sub, 0), axis=0, keepdims=True)
        idx[lo : lo + n, :] = jnp.broadcast_to(inverse, (n, 128))

    for s in range(SOL):
        for f in range(FIELDS):
            mu_a[s, f] = f_ext[f] * pat[s]
            for lo in (0, HF + CW):
                mu_b[s, f, lo : lo + HF, :] = jnp.zeros((HF, R), F32)

    def state(i):
        for k in range(1, N_OUT):
            spread[i * (N_OUT - 1) + k - 1].wait_recv()
        for side, rows in enumerate((pl.ds(0, HB), pl.ds(HB + CW, HB))):
            remote(chosen.at[i], q.at[i, :, rows, :], h_s.at[i, 0], h_r.at[i, side], (o, up)).wait_recv()

        def body(b, carry):
            rows = pl.ds(pl.multiple_of(b * 16, 16), 16)
            half = [0.5 * q[i, f, rows, :].astype(F32) for f in range(FIELDS)]
            for f in range(FIELDS):
                v = half[f] + flux_s[f, 1]
                coef[f, rows, :] = v + half[1] if f == 1 else v
            for m, e in enumerate(DIAG):
                coef[FIELDS + m, rows, :] = half[1] + flux_s[e, e]
            return carry

        lax.fori_loop(0, (CW + 2 * HB) // 16, body, 0)

    def advance(mu, s, e0, perm, co):
        near = [[mu[s, f, pl.ds(e0 + k, 8), :] for k in (-2, -1, 0, 1, 2)] for f in range(FIELDS)]
        d = [near[f][3] - near[f][1] for f in range(FIELDS)]
        new = []
        for e in range(FIELDS):
            m2, m1, m0, p1, p2 = near[e]
            v = C0 * m0 + C1 * (m1 + p1) + C2 * (m2 + p2) + jnp.take_along_axis(m0, perm, axis=1, mode="promise_in_bounds")
            for f in range(FIELDS):
                if e == 1:
                    v = v + co[f] * d[f]
                elif e == f:
                    v = v + co[FIELDS + DIAG.index(e)] * d[f]
                else:
                    v = v + flux_s[f, e] * d[f]
            new.append(v)
        return new

    def middle(i, src, dst):
        grown = UNIT ** (i + 1)

        def body(j, carry):
            e0 = 4 + 8 * j
            rows = pl.ds(e0, 8)
            perm = idx[rows, :]
            co = [coef[m, pl.ds(e0 + HB - HF, 8), :] for m in range(9)]
            fs = [f_ext[f, rows, :] * grown for f in range(FIELDS)]
            ws = [wf[f, rows, :] * (1.0 / grown) for f in range(FIELDS)]
            for s in range(SOL):
                new = advance(src, s, e0, perm, co)
                ps = pat[s, rows, :]
                acc = sacc[s]
                for f in range(FIELDS):
                    acc = acc + new[f] * ws[f]
                    dst[s, f, rows, :] = new[f] + fs[f] * ps
                sacc[s] = acc
            return carry

        lax.fori_loop(0, 17, body, 0)

    state(0)
    middle(0, mu_a, mu_b)
    state(1)
    middle(1, mu_b, mu_a)
    state(2)
    shrink = 1.0 / UNIT**STEPS

    def last(j, carry):
        e0 = HF + 8 * j
        rows = pl.ds(e0, 8)
        perm = idx[rows, :]
        co = [coef[m, pl.ds(e0 + HB - HF, 8), :] for m in range(9)]
        ws = [wf[f, rows, :] for f in range(FIELDS)]
        for s in range(SOL):
            new = advance(mu_a, s, e0, perm, co)
            acc = sacc[s]
            for f in range(FIELDS):
                v = new[f] * shrink
                acc = acc + v * ws[f]
                mu_b[s, f, rows, :] = v
            sacc[s] = acc
        return carry

    lax.fori_loop(0, CW // 8, last, 0)

    for s in range(SOL):
        sall[t, s : s + 1, :] = jnp.sum(sacc[s], axis=0, keepdims=True)
    terms = []
    for k in range(1, TILES):
        terms.append(remote(sall.at[t], sall.at[t], s_s.at[k], s_r.at[k], (o, lax.rem(t + k, TILES))))
        terms[-1].start()

    def flip(s, carry):
        for f in range(FIELDS):
            res[s, f] = mu_b[s, f, HF : HF + CW, :].T
        pltpu.make_async_copy(res.at[s], out_hbm.at[s], out_sem.at[s]).start()
        return carry

    lax.fori_loop(0, SOL, flip, 0)

    for c in terms:
        c.wait_recv()
    total = sall[0]
    for k in range(1, TILES):
        total = total + sall[k]
    total = jnp.sum(total, axis=1, keepdims=True) * (1.0 / math.sqrt(FIELDS * R * NC))
    row8 = lax.broadcasted_iota(jnp.int32, (SOL, 128), 0)
    lane8 = lax.broadcasted_iota(jnp.int32, (SOL, 128), 1)
    for g in range(GRP_DEV):
        line = jnp.sum(jnp.where(row8 == lane8 + g * AMP, total, 0.0), axis=0, keepdims=True)
        sens_ref[g : g + 1, :] = line[:, :AMP]

    for c in terms + edges + gather + spread:
        c.wait_send()
    for i in range(STEPS):

        @pl.when(lax.rem(o + 1, N_OUT) < 2)
        def _():
            for k in range(N_OUT):
                remote(chosen.at[i], q.at[i, :, pl.ds(0, HB), :], h_s.at[i, k], h_r.at[i, 0], (k, up)).wait_send()

    for s in range(SOL):
        pltpu.make_async_copy(res.at[s], out_hbm.at[s], out_sem.at[s]).wait()


def on_device(checkpoints, owner, flux_matrix, row_link, blade_group, forcing):
    smem = pl.BlockSpec(memory_space=pltpu.SMEM)
    hbm = pl.BlockSpec(memory_space=pl.ANY)
    vmem = pl.BlockSpec(memory_space=pltpu.VMEM)
    bf16 = jnp.bfloat16
    adjoint, sens = pl.pallas_call(
        kernel,
        out_shape=(
            jax.ShapeDtypeStruct((SOL, FIELDS, R, CW), F32),
            jax.ShapeDtypeStruct((GRP_DEV, AMP), F32),
        ),
        in_specs=[smem, smem, hbm, hbm, hbm, hbm, hbm],
        out_specs=(hbm, vmem),
        scratch_shapes=[
            pltpu.VMEM((FIELDS, R, CW), bf16),
            pltpu.VMEM((FIELDS, R, CW), F32),
            pltpu.VMEM((1, 128), jnp.int32),
            pltpu.VMEM((EXT, 128), F32),
            pltpu.VMEM((3, 1, R), jnp.int32),
            pltpu.VMEM((FIELDS, CW, R), bf16),
            pltpu.VMEM((N_OUT, FIELDS, CH, R), bf16),
            pltpu.VMEM((STEPS, FIELDS, CH, R), bf16),
            pltpu.VMEM((STEPS, FIELDS, CW + 2 * HB, R), bf16),
            pltpu.VMEM((FIELDS, EXT, R), F32),
            pltpu.VMEM((EXT, R), jnp.int32),
            pltpu.VMEM((9, CW + 2 * HB, R), F32),
            pltpu.VMEM((SOL, EXT, R), F32),
            pltpu.VMEM((FIELDS, EXT, R), F32),
            pltpu.VMEM((SOL, FIELDS, EXT, R), F32),
            pltpu.VMEM((SOL, FIELDS, EXT, R), F32),
            pltpu.VMEM((SOL, FIELDS, R, CW), F32),
            pltpu.VMEM((SOL, 8, 128), F32),
            pltpu.VMEM((TILES, SOL, 128), F32),
            pltpu.SemaphoreType.DMA((5,)),
            pltpu.SemaphoreType.DMA((N_OUT,)),
            pltpu.SemaphoreType.DMA((N_OUT,)),
            pltpu.SemaphoreType.DMA((STEPS, N_OUT)),
            pltpu.SemaphoreType.DMA((STEPS, N_OUT)),
            pltpu.SemaphoreType.DMA((STEPS, N_OUT)),
            pltpu.SemaphoreType.DMA((STEPS, 2)),
            pltpu.SemaphoreType.DMA((4,)),
            pltpu.SemaphoreType.DMA((4,)),
            pltpu.SemaphoreType.DMA((TILES,)),
            pltpu.SemaphoreType.DMA((TILES,)),
            pltpu.SemaphoreType.DMA((SOL,)),
        ],
        compiler_params=pltpu.CompilerParams(collective_id=0, has_side_effects=True),
    )(
        owner,
        flux_matrix,
        jnp.pad(blade_group, (0, 128 - BLADES)).reshape(1, 128),
        jnp.asarray(harmonics()),
        row_link,
        checkpoints[0],
        forcing,
    )
    return adjoint.reshape(GRP_DEV, AMP, FIELDS, R, CW), sens


def solution(mesh):
    return jax.shard_map(
        on_device,
        mesh=mesh,
        in_specs=(P("out", None, None, "blk"), P(), P(), P("blk", None), P(), P(None, None, "blk")),
        out_specs=(P("out", None, None, None, "blk"), P("out", None)),
        check_vma=False,
    )
```

```python
import functools
import math

import jax
import jax.numpy as jnp
import numpy as np
from jax import lax
from jax.experimental import pallas as pl
from jax.experimental.pallas import tpu as pltpu
from jax.sharding import PartitionSpec as P

FIELDS = 5
BLADES = 96
AMP = 4
GRP_DEV = 2
STEPS = 3
R = 128
CW = 128
TILES = 16
NC = TILES * CW
N_OUT = 8
SOL = GRP_DEV * AMP
CH = CW // N_OUT
HQ = 4
HF = 8
EXT = CW + 2 * HF

time_step = 0.25
second_diff = 0.1
fourth_diff = 0.02
link_weight = 0.5

UNIT = 1.0 / (time_step * link_weight)
C0 = UNIT * (1.0 - time_step * (2.0 * second_diff + 6.0 * fourth_diff + link_weight))
C1 = UNIT * time_step * (second_diff + 4.0 * fourth_diff)
C2 = -UNIT * time_step * fourth_diff

MESH = pl.DeviceIdType.MESH
F32 = jnp.float32
DIAG = (0, 2, 3, 4)
UNROLL = 4


def harmonics():
    c = np.arange(-HF, CW + HF)
    phase = ((c * BLADES) % NC) / NC
    rows = [
        (np.cos if a % 2 == 0 else np.sin)(2.0 * math.pi * (a // 2 + 1) * phase) for a in range(AMP)
    ]
    table = np.zeros((EXT, 128), np.float32)
    table[:, :AMP] = np.stack(rows, axis=1)
    return table


def kernel(
    owner_hbm, flux_hbm, group_hbm, harm_hbm, link_hbm, ckpt_hbm, force_hbm,
    res, sens_ref,
    owner_s, flux_s, group_s, ckpt_v, force_v, harm_v, link_v, slot, picked, q, pack, packed, edge_q, wide, f_ext, idx, coef, pat, wf, wfull,
    mu_a, mu_b, back, sacc, sall,
    in_sem, p1_s, p1_r, p2_s, p2_r, h_s, h_r, e_s, e_r, s_s, s_r,
):
    o = lax.axis_index("out")
    t = lax.axis_index("blk")
    up = lax.rem(t + 1, TILES)
    down = lax.rem(t + TILES - 1, TILES)

    loads = [
        pltpu.make_async_copy(src, dst, in_sem.at[i])
        for i, (src, dst) in enumerate(
            ((ckpt_hbm, ckpt_v), (force_hbm, force_v), (link_hbm, link_v.at[1]), (harm_hbm, harm_v),
             (group_hbm, group_s), (owner_hbm, owner_s), (flux_hbm, flux_s))
        )
    ]
    for c in loads:
        c.start()

    barrier = pltpu.get_barrier_semaphore()
    count = 0
    for k in range(1, N_OUT):
        pl.semaphore_signal(barrier, inc=1, device_id=(lax.rem(o + k, N_OUT), t), device_id_type=MESH)
        count += 1
    for side in (up, down):
        for k in range(N_OUT):
            pl.semaphore_signal(barrier, inc=1, device_id=(lax.rem(o + k, N_OUT), side), device_id_type=MESH)
            count += 1
    for k in range(2, TILES - 1):
        pl.semaphore_signal(barrier, inc=1, device_id=(o, lax.rem(t + k, TILES)), device_id_type=MESH)
        count += 1

    def remote(src, dst, send, recv, device):
        return pltpu.make_async_remote_copy(
            src_ref=src, dst_ref=dst, send_sem=send, recv_sem=recv, device_id=device, device_id_type=MESH
        )

    pack[...] = jnp.zeros_like(pack)
    loads[0].wait()
    for f in range(FIELDS):
        turned = ckpt_v[f].astype(F32).T
        for b in range(N_OUT):
            slot[b, f] = turned[b * CH : (b + 1) * CH].astype(jnp.bfloat16)
        pack[0, HQ * f : HQ * (f + 1), :] = turned[CW - HQ :]
        pack[1, HQ * f : HQ * (f + 1), :] = turned[:HQ]
    packed[...] = pack[...].astype(jnp.bfloat16)

    pl.semaphore_wait(barrier, count)

    gather = []
    for k in range(1, N_OUT):
        to = lax.rem(o + k, N_OUT)
        gather.append(remote(slot.at[to], picked.at[o], p1_s.at[k], p1_r.at[k], (to, t)))
        gather[-1].start()
    loads[1].wait()
    for f in range(FIELDS):
        f_ext[f, HF : HF + CW, :] = force_v[f].T
    loads[2].wait()
    edges = [
        remote(f_ext.at[:, pl.ds(CW, HF), :], f_ext.at[:, pl.ds(0, HF), :], e_s.at[0], e_r.at[0], (o, up)),
        remote(f_ext.at[:, pl.ds(HF, HF), :], f_ext.at[:, pl.ds(HF + CW, HF), :], e_s.at[1], e_r.at[1], (o, down)),
        remote(link_v.at[1], link_v.at[0], e_s.at[2], e_r.at[2], (o, up)),
        remote(link_v.at[1], link_v.at[2], e_s.at[3], e_r.at[3], (o, down)),
    ]
    rims = [
        remote(packed.at[side], edge_q.at[side, o], h_s.at[side, k], h_r.at[side, k], (lax.rem(o + k, N_OUT), to))
        for side, to in enumerate((up, down))
        for k in range(N_OUT)
    ]
    for c in edges + rims:
        c.start()
    for f in range(FIELDS):
        picked[o, f] = slot[o, f]

    for c in loads[3:]:
        c.wait()
    col = lax.broadcasted_iota(jnp.int32, (EXT, 128), 0) - HF
    column = lax.rem(t * CW + col + NC, NC)
    blade = lax.shift_right_logical((col + CW) * BLADES, 11)
    group_of = jnp.zeros((EXT, 128), jnp.int32)
    per = BLADES // TILES
    for b in range(per - 1, 2 * per + 1):
        group_of = jnp.where(blade == b, group_s[lax.rem(t * per + b + BLADES - per, BLADES)], group_of)
    for a in range(AMP):
        wave = jnp.broadcast_to(harm_v[:, a : a + 1], (EXT, 128))
        for g in range(GRP_DEV):
            pat[g * AMP + a] = jnp.where(group_of == o * GRP_DEV + g, wave, 0.0)
    weight = 1.0 + 2.0 * column.astype(F32) / NC

    for c in gather:
        c.wait_recv()
    spread = []
    for i, n in enumerate(reversed(range(STEPS))):
        for f in range(FIELDS):
            q[i, o, f] = picked[owner_s[n], f]
        for k in range(1, N_OUT):
            spread.append(remote(q.at[i, o], q.at[i, o], p2_s.at[i, k], p2_r.at[i, k], (lax.rem(o + k, N_OUT), t)))
            spread[-1].start()

    for c in edges:
        c.wait_recv()
    sub = lax.broadcasted_iota(jnp.int32, (R, 128), 0)
    lan = lax.broadcasted_iota(jnp.int32, (R, 128), 1)
    for side, (lo, n) in enumerate(((0, HF), (HF, CW), (HF + CW, HF))):
        links = jnp.broadcast_to(link_v[side], (R, 128)).T
        inverse = jnp.sum(jnp.where(links == lan, sub, 0), axis=0, keepdims=True)
        idx[lo : lo + n, :] = jnp.broadcast_to(inverse, (n, 128))

    for f in range(FIELDS):
        force = f_ext[f]
        weighted = force * weight
        wfull[f] = weighted
        wf[f] = jnp.where((col >= 0) & (col < CW), weighted, 0.0)
        for s in range(SOL):
            mu_a[s, f] = force * pat[s]
    inner = wf[0, HF : HF + CW] * f_ext[0, HF : HF + CW]
    for f in range(1, FIELDS):
        inner = inner + wf[f, HF : HF + CW] * f_ext[f, HF : HF + CW]
    for s in range(SOL):
        start = (-2.0 * inner) * pat[s, HF : HF + CW]
        sacc[s] = jnp.sum(start.reshape(CW // 8, 8, 128), axis=0)
        for f in range(FIELDS):
            for lo in (0, HF + CW):
                mu_b[s, f, lo : lo + HF, :] = jnp.zeros((HF, R), F32)

    def stencil(m2, m1, m0, p1, p2, perm):
        moved = jnp.take_along_axis(m0, perm, axis=1, mode="promise_in_bounds")
        return C0 * m0 + C1 * (m1 + p1) + C2 * (m2 + p2) + moved

    def advance(mu, s, e0, perm, mix):
        near = [[mu[s, f, pl.ds(e0 + k, 8), :] for k in (-2, -1, 0, 1, 2)] for f in range(FIELDS)]
        d = [near[f][3] - near[f][1] for f in range(FIELDS)]
        new = []
        for e in range(FIELDS):
            v = stencil(*near[e], perm)
            for f in range(FIELDS):
                v = v + mix(f, e) * d[f]
            new.append(v)
        return new

    def constant(f, e):
        return flux_s[f, e]

    def mixed(co):
        def mix(f, e):
            if e == 1:
                return co[f]
            return co[FIELDS + DIAG.index(e)] if e == f else flux_s[f, e]

        return mix

    def early(j, carry):
        e0 = 4 + 8 * j
        rows = pl.ds(e0, 8)
        perm = idx[rows, :]
        fs = [f_ext[f, rows, :] * UNIT for f in range(FIELDS)]

        def some(p, carry):
            for r in range(UNROLL):
                s = p * UNROLL + r
                new = advance(mu_a, s, e0, perm, constant)
                ps = pat[s, rows, :]
                for f in range(FIELDS):
                    mu_b[s, f, rows, :] = new[f] + fs[f] * ps
            return carry

        return lax.fori_loop(0, SOL // UNROLL, some, carry)

    lax.fori_loop(0, 17, early, 0)

    def state(i, n, write):
        for k in range(1, N_OUT):
            spread[i * (N_OUT - 1) + k - 1].wait_recv()

        def body(b, carry):
            write(pl.ds(pl.multiple_of(HF + b * CH, 8), CH), [0.5 * q[i, b, f].astype(F32) for f in range(FIELDS)])
            return carry

        lax.fori_loop(0, N_OUT, body, 0)
        for side, lo in enumerate((HF - HQ, HF + CW)):
            wide[...] = edge_q[side, owner_s[n]].astype(F32)
            write(pl.ds(lo, HQ), [0.5 * wide[HQ * f : HQ * (f + 1), :] for f in range(FIELDS)])

    def halves(rows, half):
        for f in range(FIELDS):
            coef[f, rows, :] = half[f]

    def blocks(rows, half):
        for f in range(FIELDS):
            v = half[f] + flux_s[f, 1]
            coef[f, rows, :] = v + half[1] if f == 1 else v
        for m, e in enumerate(DIAG):
            coef[FIELDS + m, rows, :] = half[1] + flux_s[e, e]

    for c in rims:
        c.wait_recv()
    state(0, 2, halves)

    def finish(j, carry):
        e0 = 4 + 8 * j
        rows = pl.ds(e0, 8)
        half = [coef[f, rows, :] for f in range(FIELDS)]
        ws = [wf[f, rows, :] * (1.0 / UNIT) for f in range(FIELDS)]
        for s in range(SOL):
            d = [mu_a[s, f, pl.ds(e0 + 1, 8), :] - mu_a[s, f, pl.ds(e0 - 1, 8), :] for f in range(FIELDS)]
            dot = half[0] * d[0]
            for f in range(1, FIELDS):
                dot = dot + half[f] * d[f]
            acc = sacc[s]
            for f in range(FIELDS):
                v = mu_b[s, f, rows, :] + half[1] * d[f]
                if f == 1:
                    v = v + dot
                mu_b[s, f, rows, :] = v
                acc = acc + v * ws[f]
            sacc[s] = acc
        return carry

    lax.fori_loop(0, 17, finish, 0)

    state(1, 1, blocks)

    def second(j, carry):
        e0 = 4 + 8 * j
        rows = pl.ds(e0, 8)
        perm = idx[rows, :]
        mix = mixed([coef[m, rows, :] for m in range(9)])
        fs = [f_ext[f, rows, :] * UNIT**2 for f in range(FIELDS)]

        def some(p, carry):
            for r in range(UNROLL):
                s = p * UNROLL + r
                new = advance(mu_b, s, e0, perm, mix)
                ps = pat[s, rows, :]
                for f in range(FIELDS):
                    mu_a[s, f, rows, :] = new[f] + fs[f] * ps
            return carry

        return lax.fori_loop(0, SOL // UNROLL, some, carry)

    lax.fori_loop(0, 17, second, 0)

    state(2, 0, blocks)

    def turn(j, carry):
        rows = pl.ds(4 + 8 * j, 8)
        mix = mixed([coef[m, rows, :] for m in range(9)])
        v = [wfull[e, rows, :] for e in range(FIELDS)]
        for f in range(FIELDS):
            w = mix(f, 0) * v[0]
            for e in range(1, FIELDS):
                w = w + mix(f, e) * v[e]
            back[f, rows, :] = w
        return carry

    lax.fori_loop(0, 17, turn, 0)

    def weigh(j, carry):
        e0 = pl.multiple_of(HF + 8 * j, 8)
        rows = pl.ds(e0, 8)
        perm = jnp.broadcast_to(link_v[1], (8, 128))
        ws = []
        for f in range(FIELDS):
            near = [wfull[f, pl.ds(e0 + k, 8), :] for k in (-2, -1, 0, 1, 2)]
            v = stencil(*near, perm) + back[f, pl.ds(e0 - 1, 8), :] - back[f, pl.ds(e0 + 1, 8), :]
            ws.append(near[2] * UNIT**-2 + v * UNIT**-3)
        for s in range(SOL):
            acc = sacc[s]
            for f in range(FIELDS):
                acc = acc + mu_a[s, f, rows, :] * ws[f]
            sacc[s] = acc
        return carry

    lax.fori_loop(0, CW // 8, weigh, 0)

    for s in range(SOL):
        sall[t, s : s + 1, :] = jnp.sum(sacc[s], axis=0, keepdims=True)
    terms = []
    for k in range(1, TILES):
        terms.append(remote(sall.at[t], sall.at[t], s_s.at[k], s_r.at[k], (o, lax.rem(t + k, TILES))))
        terms[-1].start()

    def third(s, carry):
        def some(p, carry):
            for r in range(UNROLL):
                e0 = pl.multiple_of(HF + 8 * (p * UNROLL + r), 8)
                rows = pl.ds(e0, 8)
                new = advance(mu_a, s, e0, idx[rows, :], mixed([coef[m, rows, :] for m in range(9)]))
                for f in range(FIELDS):
                    res[s, f, pl.ds(pl.multiple_of(e0 - HF, 8), 8), :] = new[f] * UNIT**-3
            return carry

        lax.fori_loop(0, CW // 8 // UNROLL, some, 0)
        return carry

    lax.fori_loop(0, SOL, third, 0)

    for c in terms:
        c.wait_recv()
    total = sall[0]
    for k in range(1, TILES):
        total = total + sall[k]
    total = jnp.sum(total, axis=1, keepdims=True) * (1.0 / math.sqrt(FIELDS * R * NC))
    row8 = lax.broadcasted_iota(jnp.int32, (SOL, 128), 0)
    lane8 = lax.broadcasted_iota(jnp.int32, (SOL, 128), 1)
    for g in range(GRP_DEV):
        line = jnp.sum(jnp.where(row8 == lane8 + g * AMP, total, 0.0), axis=0, keepdims=True)
        sens_ref[g : g + 1, :] = line[:, :AMP]

    for c in terms + edges + rims + gather + spread:
        c.wait_send()


def flip(turned_ref, sens_ref, out_hbm, sens_out, res, sem):
    sens_out[...] = sens_ref[...]
    copies = [pltpu.make_async_copy(res.at[s], out_hbm.at[s], sem.at[s]) for s in range(SOL)]
    for s in range(SOL):
        for f in range(FIELDS):
            res[s, f] = turned_ref[s, f].T
        copies[s].start()
    for c in copies:
        c.wait()


def on_device(checkpoints, owner, flux_matrix, row_link, blade_group, forcing):
    hbm = pl.BlockSpec(memory_space=pltpu.HBM)
    vmem = pl.BlockSpec(memory_space=pltpu.VMEM)
    bf16 = jnp.bfloat16
    dma = pltpu.SemaphoreType.DMA
    shapes = (
        jax.ShapeDtypeStruct((SOL, FIELDS, R, CW), F32),
        jax.ShapeDtypeStruct((GRP_DEV, AMP), F32),
    )
    turned, sens = pl.pallas_call(
        kernel,
        out_shape=shapes,
        in_specs=[hbm] * 7,
        out_specs=(vmem, vmem),
        scratch_shapes=[
            pltpu.SMEM((N_OUT,), jnp.int32),
            pltpu.SMEM((FIELDS, FIELDS), F32),
            pltpu.SMEM((BLADES,), jnp.int32),
            pltpu.VMEM((FIELDS, R, CW), bf16),
            pltpu.VMEM((FIELDS, R, CW), F32),
            pltpu.VMEM((EXT, 128), F32),
            pltpu.VMEM((3, 1, R), jnp.int32),
            pltpu.VMEM((N_OUT, FIELDS, CH, R), bf16),
            pltpu.VMEM((N_OUT, FIELDS, CH, R), bf16),
            pltpu.VMEM((STEPS, N_OUT, FIELDS, CH, R), bf16),
            pltpu.VMEM((2, 32, R), F32),
            pltpu.VMEM((2, 32, R), bf16),
            pltpu.VMEM((2, N_OUT, 32, R), bf16),
            pltpu.VMEM((32, R), F32),
            pltpu.VMEM((FIELDS, EXT, R), F32),
            pltpu.VMEM((EXT, R), jnp.int32),
            pltpu.VMEM((9, EXT, R), F32),
            pltpu.VMEM((SOL, EXT, R), F32),
            pltpu.VMEM((FIELDS, EXT, R), F32),
            pltpu.VMEM((FIELDS, EXT, R), F32),
            pltpu.VMEM((SOL, FIELDS, EXT, R), F32),
            pltpu.VMEM((SOL, FIELDS, EXT, R), F32),
            pltpu.VMEM((FIELDS, EXT, R), F32),
            pltpu.VMEM((SOL, 8, 128), F32),
            pltpu.VMEM((TILES, SOL, 128), F32),
            dma((7,)),
            dma((N_OUT,)),
            dma((N_OUT,)),
            dma((STEPS, N_OUT)),
            dma((STEPS, N_OUT)),
            dma((2, N_OUT)),
            dma((2, N_OUT)),
            dma((4,)),
            dma((4,)),
            dma((TILES,)),
            dma((TILES,)),
        ],
        compiler_params=pltpu.CompilerParams(collective_id=0, has_side_effects=True, vmem_limit_bytes=24 << 20),
    )(
        *(
            pltpu.with_memory_space_constraint(x, pltpu.HBM)
            for x in (owner, flux_matrix, blade_group, jnp.asarray(harmonics()), row_link, checkpoints[0], forcing)
        )
    )
    adjoint, sens = pl.pallas_call(
        flip,
        out_shape=shapes,
        in_specs=[vmem, vmem],
        out_specs=(hbm, vmem),
        scratch_shapes=[pltpu.VMEM((SOL, FIELDS, R, CW), F32), dma((SOL,))],
        compiler_params=pltpu.CompilerParams(vmem_limit_bytes=8 << 20),
    )(turned, sens)
    return adjoint.reshape(GRP_DEV, AMP, FIELDS, R, CW), sens


def solution(mesh):
    return jax.shard_map(
        on_device,
        mesh=mesh,
        in_specs=(P("out", None, None, "blk"), P(), P(), P("blk", None), P(), P(None, None, "blk")),
        out_specs=(P("out", None, None, None, "blk"), P("out", None)),
        check_vma=False,
    )
```

```python
import functools
import math

import jax
import jax.numpy as jnp
import numpy as np
from jax import lax
from jax.experimental import pallas as pl
from jax.experimental.pallas import tpu as pltpu
from jax.sharding import PartitionSpec as P

FIELDS = 5
BLADES = 96
AMP = 4
GRP_DEV = 2
STEPS = 3
R = 128
CW = 128
TILES = 16
NC = TILES * CW
N_OUT = 8
SOL = GRP_DEV * AMP
CH = CW // N_OUT
HQ = 5
HF = 8
EXT = CW + 2 * HF

time_step = 0.25
second_diff = 0.1
fourth_diff = 0.02
link_weight = 0.5

UNIT = 1.0 / (time_step * link_weight)
C0 = UNIT * (1.0 - time_step * (2.0 * second_diff + 6.0 * fourth_diff + link_weight))
C1 = UNIT * time_step * (second_diff + 4.0 * fourth_diff)
C2 = -UNIT * time_step * fourth_diff

MESH = pl.DeviceIdType.MESH
F32 = jnp.float32
DIAG = (0, 2, 3, 4)
UNROLL = 8
PAIR = 6
WIDE = 8


def harmonics():
    c = np.arange(-HF, CW + HF)
    phase = ((c * BLADES) % NC) / NC
    rows = [
        (np.cos if a % 2 == 0 else np.sin)(2.0 * math.pi * (a // 2 + 1) * phase) for a in range(AMP)
    ]
    table = np.zeros((EXT, 128), np.float32)
    table[:, :AMP] = np.stack(rows, axis=1)
    return table


def kernel(
    owner_hbm, flux_hbm, group_hbm, harm_hbm, link_hbm, ckpt_hbm, force_hbm,
    res, sens_ref,
    owner_s, flux_s, group_s, ckpt_v, force_v, harm_v, link_v, slot, picked, q, pack, packed, edge_q, wide, f_ext, idx, idx_t, coef, halves, pat, wf, dual,
    mu_a, mu_b, back, sall,
    in_sem, p1_s, p1_r, p2_s, p2_r, h_s, h_r, e_s, e_r, s_s, s_r,
):
    o = lax.axis_index("out")
    t = lax.axis_index("blk")
    up = lax.rem(t + 1, TILES)
    down = lax.rem(t + TILES - 1, TILES)

    loads = [
        pltpu.make_async_copy(src, dst, in_sem.at[i])
        for i, (src, dst) in enumerate(
            ((ckpt_hbm, ckpt_v), (force_hbm, force_v), (link_hbm, link_v.at[1]), (harm_hbm, harm_v),
             (group_hbm, group_s), (owner_hbm, owner_s), (flux_hbm, flux_s))
        )
    ]
    for c in loads:
        c.start()

    barrier = pltpu.get_barrier_semaphore()
    count = 0
    for k in range(1, N_OUT):
        pl.semaphore_signal(barrier, inc=1, device_id=(lax.rem(o + k, N_OUT), t), device_id_type=MESH)
        count += 1
    for side in (up, down):
        for k in range(N_OUT):
            pl.semaphore_signal(barrier, inc=1, device_id=(lax.rem(o + k, N_OUT), side), device_id_type=MESH)
            count += 1
    for k in range(2, TILES - 1):
        pl.semaphore_signal(barrier, inc=1, device_id=(o, lax.rem(t + k, TILES)), device_id_type=MESH)
        count += 1

    def remote(src, dst, send, recv, device):
        return pltpu.make_async_remote_copy(
            src_ref=src, dst_ref=dst, send_sem=send, recv_sem=recv, device_id=device, device_id_type=MESH
        )

    pack[...] = jnp.zeros_like(pack)
    loads[0].wait()
    for f in range(FIELDS):
        turned = ckpt_v[f].astype(F32).T
        for b in range(N_OUT):
            slot[b, f] = turned[b * CH : (b + 1) * CH].astype(jnp.bfloat16)
        pack[0, HQ * f : HQ * (f + 1), :] = turned[CW - HQ :]
        pack[1, HQ * f : HQ * (f + 1), :] = turned[:HQ]
    packed[...] = pack[...].astype(jnp.bfloat16)

    pl.semaphore_wait(barrier, count)

    gather = []
    for k in range(1, N_OUT):
        to = lax.rem(o + k, N_OUT)
        gather.append(remote(slot.at[to], picked.at[o], p1_s.at[k], p1_r.at[k], (to, t)))
        gather[-1].start()
    loads[1].wait()
    for f in range(FIELDS):
        f_ext[f, HF : HF + CW, :] = force_v[f].T
    loads[2].wait()
    edges = [
        remote(f_ext.at[:, pl.ds(CW, HF), :], f_ext.at[:, pl.ds(0, HF), :], e_s.at[0], e_r.at[0], (o, up)),
        remote(f_ext.at[:, pl.ds(HF, HF), :], f_ext.at[:, pl.ds(HF + CW, HF), :], e_s.at[1], e_r.at[1], (o, down)),
        remote(link_v.at[1], link_v.at[0], e_s.at[2], e_r.at[2], (o, up)),
        remote(link_v.at[1], link_v.at[2], e_s.at[3], e_r.at[3], (o, down)),
    ]
    rims = [
        remote(packed.at[side], edge_q.at[side, o], h_s.at[side, k], h_r.at[side, k], (lax.rem(o + k, N_OUT), to))
        for side, to in enumerate((up, down))
        for k in range(N_OUT)
    ]
    for c in edges + rims:
        c.start()
    for f in range(FIELDS):
        picked[o, f] = slot[o, f]

    for c in loads[3:]:
        c.wait()
    col = lax.broadcasted_iota(jnp.int32, (EXT, 128), 0) - HF
    column = lax.rem(t * CW + col + NC, NC)
    blade = lax.shift_right_logical((col + CW) * BLADES, 11)
    group_of = jnp.zeros((EXT, 128), jnp.int32)
    per = BLADES // TILES
    for b in range(per - 1, 2 * per + 1):
        group_of = jnp.where(blade == b, group_s[lax.rem(t * per + b + BLADES - per, BLADES)], group_of)
    for a in range(AMP):
        wave = jnp.broadcast_to(harm_v[:, a : a + 1], (EXT, 128))
        for g in range(GRP_DEV):
            pat[g * AMP + a] = jnp.where(group_of == o * GRP_DEV + g, wave, 0.0)
    weight = 1.0 + 2.0 * column.astype(F32) / NC

    for c in gather:
        c.wait_recv()
    spread = []
    for i in range(STEPS):
        for f in range(FIELDS):
            q[i, o, f] = picked[owner_s[i], f]
        for k in range(1, N_OUT):
            spread.append(remote(q.at[i, o], q.at[i, o], p2_s.at[i, k], p2_r.at[i, k], (lax.rem(o + k, N_OUT), t)))
            spread[-1].start()

    for c in edges:
        c.wait_recv()
    sub = lax.broadcasted_iota(jnp.int32, (R, 128), 0)
    lan = lax.broadcasted_iota(jnp.int32, (R, 128), 1)
    for side, (lo, n) in enumerate(((0, HF), (HF, CW), (HF + CW, HF))):
        links = jnp.broadcast_to(link_v[side], (R, 128)).T
        inverse = jnp.sum(jnp.where(links == lan, sub, 0), axis=0, keepdims=True)
        idx[lo : lo + n, :] = jnp.broadcast_to(inverse, (n, 128))
        idx_t[lo : lo + n, :] = jnp.broadcast_to(link_v[side], (n, 128))

    for f in range(FIELDS):
        force = f_ext[f]
        wf[f] = force * weight
        for s in range(SOL):
            mu_a[s, f] = force * pat[s]
    for lo in (0, HF + CW):
        for f in range(FIELDS):
            for m in range(2):
                dual[m, f, lo : lo + HF, :] = jnp.zeros((HF, R), F32)
            for s in range(SOL):
                mu_b[s, f, lo : lo + HF, :] = jnp.zeros((HF, R), F32)

    def stencil(m2, m1, m0, p1, p2, perm):
        moved = jnp.take_along_axis(m0, perm, axis=1, mode="promise_in_bounds")
        return C0 * m0 + C1 * (m1 + p1) + C2 * (m2 + p2) + moved

    def advance(mu, s, e0, perm, mix):
        near = [[mu[s, f, pl.ds(e0 + k, 8), :] for k in (-2, -1, 0, 1, 2)] for f in range(FIELDS)]
        d = [near[f][3] - near[f][1] for f in range(FIELDS)]
        new = []
        for e in range(FIELDS):
            v = stencil(*near[e], perm)
            for f in range(FIELDS):
                v = v + mix(f, e) * d[f]
            new.append(v)
        return new

    def constant(f, e):
        return flux_s[f, e]

    def mixed(co):
        def mix(f, e):
            if e == 1:
                return co[f]
            return co[FIELDS + DIAG.index(e)] if e == f else flux_s[f, e]

        return mix

    def early(j, carry):
        e0 = 4 + 8 * j
        rows = pl.ds(e0, 8)
        perm = idx[rows, :]
        fs = [f_ext[f, rows, :] * UNIT for f in range(FIELDS)]

        def some(p, carry):
            for r in range(UNROLL):
                s = p * UNROLL + r
                new = advance(mu_a, s, e0, perm, constant)
                ps = pat[s, rows, :]
                for f in range(FIELDS):
                    mu_b[s, f, rows, :] = new[f] + fs[f] * ps
            return carry

        return lax.fori_loop(0, SOL // UNROLL, some, carry)

    lax.fori_loop(0, 17, early, 0)

    def state(n):
        for k in range(1, N_OUT):
            spread[n * (N_OUT - 1) + k - 1].wait_recv()

        def write(rows, half):
            for f in range(FIELDS):
                v = half[f] + flux_s[f, 1]
                coef[n, f, rows, :] = v + half[1] if f == 1 else v
            for m, e in enumerate(DIAG):
                coef[n, FIELDS + m, rows, :] = half[1] + flux_s[e, e]
            if n == STEPS - 1:
                for f in range(FIELDS):
                    halves[f, rows, :] = half[f]

        def body(b, carry):
            write(pl.ds(pl.multiple_of(HF + b * CH, 8), CH), [0.5 * q[n, b, f].astype(F32) for f in range(FIELDS)])
            return carry

        lax.fori_loop(0, N_OUT, body, 0)
        for side, lo in enumerate((HF - HQ, HF + CW)):
            wide[...] = edge_q[side, owner_s[n]].astype(F32)
            write(pl.ds(lo, HQ), [0.5 * wide[HQ * f : HQ * (f + 1), :] for f in range(FIELDS)])

    for c in rims:
        c.wait_recv()

    def turn(n, x):
        def body(j, carry):
            for r in range(PAIR):
                rows = pl.ds(jnp.minimum(HF - HQ + 8 * (j * PAIR + r), HF + CW + HQ - 8), 8)
                mix = mixed([coef[n, m, rows, :] for m in range(9)])
                v = [x[e, rows, :] for e in range(FIELDS)]
                for f in range(FIELDS):
                    w = mix(f, 0) * v[0]
                    for e in range(1, FIELDS):
                        w = w + mix(f, e) * v[e]
                    back[f, rows, :] = w
            return carry

        lax.fori_loop(0, 18 // PAIR, body, 0)

    def adjoint_at(x, f, e0):
        near = [x[f, pl.ds(e0 + k, 8), :] for k in (-2, -1, 0, 1, 2)]
        w = back[f, pl.ds(e0 - 1, 8), :] - back[f, pl.ds(e0 + 1, 8), :]
        return (stencil(*near, idx_t[pl.ds(e0, 8), :]) + w) * (1.0 / UNIT)

    def push(n, x, to):
        state(n)
        turn(n, x)

        def body(j, carry):
            for r in range(PAIR):
                e0 = jnp.minimum(4 + 8 * (j * PAIR + r), HF + CW - 4)
                for f in range(FIELDS):
                    to[f, pl.ds(e0, 8), :] = wf[f, pl.ds(e0, 8), :] + adjoint_at(x, f, e0)
            return carry

        lax.fori_loop(0, 18 // PAIR, body, 0)

    push(0, wf, dual.at[0])
    push(1, dual.at[0], dual.at[1])
    state(2)
    turn(2, dual.at[1])

    def weigh(j, sums):
        for r in range(WIDE):
            e0 = pl.multiple_of(HF + 8 * (j * WIDE + r), 8)
            rows = pl.ds(e0, 8)
            p = None
            for f in range(FIELDS):
                v = dual[0, f, rows, :] + dual[1, f, rows, :] - 2.0 * wf[f, rows, :] + adjoint_at(dual.at[1], f, e0)
                v = v * f_ext[f, rows, :]
                p = v if p is None else p + v
            sums = tuple(sums[s] + p * pat[s, rows, :] for s in range(SOL))
        return sums

    sums = lax.fori_loop(0, CW // 8 // WIDE, weigh, (jnp.zeros((8, 128), F32),) * SOL)

    for s in range(SOL):
        sall[t, s : s + 1, :] = jnp.sum(sums[s], axis=0, keepdims=True)
    terms = []
    for k in range(1, TILES):
        terms.append(remote(sall.at[t], sall.at[t], s_s.at[k], s_r.at[k], (o, lax.rem(t + k, TILES))))
        terms[-1].start()

    def finish(j, carry):
        e0 = 4 + 8 * j
        rows = pl.ds(e0, 8)
        half = [halves[f, rows, :] for f in range(FIELDS)]
        for s in range(SOL):
            d = [mu_a[s, f, pl.ds(e0 + 1, 8), :] - mu_a[s, f, pl.ds(e0 - 1, 8), :] for f in range(FIELDS)]
            dot = half[0] * d[0]
            for f in range(1, FIELDS):
                dot = dot + half[f] * d[f]
            for f in range(FIELDS):
                v = mu_b[s, f, rows, :] + half[1] * d[f]
                mu_b[s, f, rows, :] = v + dot if f == 1 else v
        return carry

    lax.fori_loop(0, 17, finish, 0)

    def second(j, carry):
        e0 = 4 + 8 * j
        rows = pl.ds(e0, 8)
        perm = idx[rows, :]
        mix = mixed([coef[1, m, rows, :] for m in range(9)])
        fs = [f_ext[f, rows, :] * UNIT**2 for f in range(FIELDS)]

        def some(p, carry):
            for r in range(UNROLL):
                s = p * UNROLL + r
                new = advance(mu_b, s, e0, perm, mix)
                ps = pat[s, rows, :]
                for f in range(FIELDS):
                    mu_a[s, f, rows, :] = new[f] + fs[f] * ps
            return carry

        return lax.fori_loop(0, SOL // UNROLL, some, carry)

    lax.fori_loop(0, 17, second, 0)

    def third(s, carry):
        def some(p, carry):
            for r in range(UNROLL):
                e0 = pl.multiple_of(HF + 8 * (p * UNROLL + r), 8)
                rows = pl.ds(e0, 8)
                new = advance(mu_a, s, e0, idx[rows, :], mixed([coef[0, m, rows, :] for m in range(9)]))
                for f in range(FIELDS):
                    res[s, f, pl.ds(pl.multiple_of(e0 - HF, 8), 8), :] = new[f] * UNIT**-3
            return carry

        lax.fori_loop(0, CW // 8 // UNROLL, some, 0)
        return carry

    lax.fori_loop(0, SOL, third, 0)

    for c in terms:
        c.wait_recv()
    total = sall[0]
    for k in range(1, TILES):
        total = total + sall[k]
    total = jnp.sum(total, axis=1, keepdims=True) * (1.0 / math.sqrt(FIELDS * R * NC))
    row8 = lax.broadcasted_iota(jnp.int32, (SOL, 128), 0)
    lane8 = lax.broadcasted_iota(jnp.int32, (SOL, 128), 1)
    for g in range(GRP_DEV):
        line = jnp.sum(jnp.where(row8 == lane8 + g * AMP, total, 0.0), axis=0, keepdims=True)
        sens_ref[g : g + 1, :] = line[:, :AMP]

    for c in terms + edges + rims + gather + spread:
        c.wait_send()


def flip(turned_ref, sens_ref, out_hbm, sens_out, res, sem):
    sens_out[...] = sens_ref[...]
    copies = [pltpu.make_async_copy(res.at[s], out_hbm.at[s], sem.at[s]) for s in range(SOL)]
    for s in range(SOL):
        for f in range(FIELDS):
            res[s, f] = turned_ref[s, f].T
        copies[s].start()
    for c in copies:
        c.wait()


def on_device(checkpoints, owner, flux_matrix, row_link, blade_group, forcing):
    hbm = pl.BlockSpec(memory_space=pltpu.HBM)
    vmem = pl.BlockSpec(memory_space=pltpu.VMEM)
    bf16 = jnp.bfloat16
    dma = pltpu.SemaphoreType.DMA
    shapes = (
        jax.ShapeDtypeStruct((SOL, FIELDS, R, CW), F32),
        jax.ShapeDtypeStruct((GRP_DEV, AMP), F32),
    )
    turned, sens = pl.pallas_call(
        kernel,
        out_shape=shapes,
        in_specs=[hbm] * 7,
        out_specs=(vmem, vmem),
        scratch_shapes=[
            pltpu.SMEM((N_OUT,), jnp.int32),
            pltpu.SMEM((FIELDS, FIELDS), F32),
            pltpu.SMEM((BLADES,), jnp.int32),
            pltpu.VMEM((FIELDS, R, CW), bf16),
            pltpu.VMEM((FIELDS, R, CW), F32),
            pltpu.VMEM((EXT, 128), F32),
            pltpu.VMEM((3, 1, R), jnp.int32),
            pltpu.VMEM((N_OUT, FIELDS, CH, R), bf16),
            pltpu.VMEM((N_OUT, FIELDS, CH, R), bf16),
            pltpu.VMEM((STEPS, N_OUT, FIELDS, CH, R), bf16),
            pltpu.VMEM((2, 32, R), F32),
            pltpu.VMEM((2, 32, R), bf16),
            pltpu.VMEM((2, N_OUT, 32, R), bf16),
            pltpu.VMEM((32, R), F32),
            pltpu.VMEM((FIELDS, EXT, R), F32),
            pltpu.VMEM((EXT, R), jnp.int32),
            pltpu.VMEM((EXT, R), jnp.int32),
            pltpu.VMEM((STEPS, 9, EXT, R), F32),
            pltpu.VMEM((FIELDS, EXT, R), F32),
            pltpu.VMEM((SOL, EXT, R), F32),
            pltpu.VMEM((FIELDS, EXT, R), F32),
            pltpu.VMEM((2, FIELDS, EXT, R), F32),
            pltpu.VMEM((SOL, FIELDS, EXT, R), F32),
            pltpu.VMEM((SOL, FIELDS, EXT, R), F32),
            pltpu.VMEM((FIELDS, EXT, R), F32),
            pltpu.VMEM((TILES, SOL, 128), F32),
            dma((7,)),
            dma((N_OUT,)),
            dma((N_OUT,)),
            dma((STEPS, N_OUT)),
            dma((STEPS, N_OUT)),
            dma((2, N_OUT)),
            dma((2, N_OUT)),
            dma((4,)),
            dma((4,)),
            dma((TILES,)),
            dma((TILES,)),
        ],
        compiler_params=pltpu.CompilerParams(collective_id=0, has_side_effects=True, vmem_limit_bytes=24 << 20),
    )(
        *(
            pltpu.with_memory_space_constraint(x, pltpu.HBM)
            for x in (owner, flux_matrix, blade_group, jnp.asarray(harmonics()), row_link, checkpoints[0], forcing)
        )
    )
    adjoint, sens = pl.pallas_call(
        flip,
        out_shape=shapes,
        in_specs=[vmem, vmem],
        out_specs=(hbm, vmem),
        scratch_shapes=[pltpu.VMEM((SOL, FIELDS, R, CW), F32), dma((SOL,))],
        compiler_params=pltpu.CompilerParams(vmem_limit_bytes=8 << 20),
    )(turned, sens)
    return adjoint.reshape(GRP_DEV, AMP, FIELDS, R, CW), sens


def solution(mesh):
    return jax.shard_map(
        on_device,
        mesh=mesh,
        in_specs=(P("out", None, None, "blk"), P(), P(), P("blk", None), P(), P(None, None, "blk")),
        out_specs=(P("out", None, None, None, "blk"), P("out", None)),
        check_vma=False,
    )
```

```python
import functools
import math

import jax
import jax.numpy as jnp
import numpy as np
from jax import lax
from jax.experimental import pallas as pl
from jax.experimental.pallas import tpu as pltpu
from jax.sharding import PartitionSpec as P

FIELDS = 5
BLADES = 96
AMP = 4
GRP_DEV = 2
STEPS = 3
R = 128
CW = 128
TILES = 16
NC = TILES * CW
N_OUT = 8
SOL = GRP_DEV * AMP
CH = CW // N_OUT
HQ = 5
HF = 8
EXT = CW + 2 * HF

time_step = 0.25
second_diff = 0.1
fourth_diff = 0.02
link_weight = 0.5

UNIT = 1.0 / (time_step * link_weight)
C0 = UNIT * (1.0 - time_step * (2.0 * second_diff + 6.0 * fourth_diff + link_weight))
C1 = UNIT * time_step * (second_diff + 4.0 * fourth_diff)
C2 = -UNIT * time_step * fourth_diff

MESH = pl.DeviceIdType.MESH
F32 = jnp.float32
DIAG = (0, 2, 3, 4)
UNROLL = 8
ORDER = (5, 3, 7, 4, 1, 2, 6)
PAIR = 6
WIDE = 8


def harmonics():
    c = np.arange(-HF, CW + HF)
    phase = ((c * BLADES) % NC) / NC
    rows = [
        (np.cos if a % 2 == 0 else np.sin)(2.0 * math.pi * (a // 2 + 1) * phase) for a in range(AMP)
    ]
    table = np.zeros((EXT, 128), np.float32)
    table[:, :AMP] = np.stack(rows, axis=1)
    return table


def kernel(
    owner_hbm, flux_hbm, group_hbm, harm_hbm, link_hbm, ckpt_hbm, force_hbm,
    res, sens_ref,
    owner_s, flux_s, group_s, ckpt_v, force_v, harm_v, link_v, slot, picked, q, pack, packed, edge_q, wide, f_ext, idx, idx_t, coef, halves, pat, wf, dual,
    mu_a, mu_b, src, back, sall,
    in_sem, p1_s, p1_r, p2_s, p2_r, h_s, h_r, e_s, e_r, s_s, s_r,
):
    o = lax.axis_index("out")
    t = lax.axis_index("blk")
    up = lax.rem(t + 1, TILES)

    def peer(k):
        return lax.rem(o // 2 + k // 2, N_OUT // 2) * 2 + lax.rem(o + k, 2)

    down = lax.rem(t + TILES - 1, TILES)

    loads = [
        pltpu.make_async_copy(src, dst, in_sem.at[i])
        for i, (src, dst) in enumerate(
            ((ckpt_hbm, ckpt_v), (force_hbm, force_v), (link_hbm, link_v.at[1]), (harm_hbm, harm_v),
             (group_hbm, group_s), (owner_hbm, owner_s), (flux_hbm, flux_s))
        )
    ]
    for c in loads:
        c.start()

    barrier = pltpu.get_barrier_semaphore()
    count = 0
    for k in range(1, N_OUT):
        pl.semaphore_signal(barrier, inc=1, device_id=(lax.rem(o + k, N_OUT), t), device_id_type=MESH)
        count += 1
    for side in (up, down):
        for k in range(N_OUT):
            pl.semaphore_signal(barrier, inc=1, device_id=(lax.rem(o + k, N_OUT), side), device_id_type=MESH)
            count += 1
    for k in range(2, TILES - 1):
        pl.semaphore_signal(barrier, inc=1, device_id=(o, lax.rem(t + k, TILES)), device_id_type=MESH)
        count += 1

    def remote(src, dst, send, recv, device):
        return pltpu.make_async_remote_copy(
            src_ref=src, dst_ref=dst, send_sem=send, recv_sem=recv, device_id=device, device_id_type=MESH
        )

    pack[...] = jnp.zeros_like(pack)
    loads[0].wait()
    for f in range(FIELDS):
        turned = ckpt_v[f].astype(F32).T
        for b in range(N_OUT):
            slot[b, f] = turned[b * CH : (b + 1) * CH].astype(jnp.bfloat16)
        pack[0, HQ * f : HQ * (f + 1), :] = turned[CW - HQ :]
        pack[1, HQ * f : HQ * (f + 1), :] = turned[:HQ]
    packed[...] = pack[...].astype(jnp.bfloat16)

    pl.semaphore_wait(barrier, count)

    gather = []
    for k in ORDER:
        to = peer(k)
        gather.append(remote(slot.at[to], picked.at[o], p1_s.at[k], p1_r.at[k], (to, t)))
        gather[-1].start()
    loads[1].wait()
    for f in range(FIELDS):
        f_ext[f, HF : HF + CW, :] = force_v[f].T
    loads[2].wait()
    edges = [
        remote(f_ext.at[:, pl.ds(CW, HF), :], f_ext.at[:, pl.ds(0, HF), :], e_s.at[0], e_r.at[0], (o, up)),
        remote(f_ext.at[:, pl.ds(HF, HF), :], f_ext.at[:, pl.ds(HF + CW, HF), :], e_s.at[1], e_r.at[1], (o, down)),
        remote(link_v.at[1], link_v.at[0], e_s.at[2], e_r.at[2], (o, up)),
        remote(link_v.at[1], link_v.at[2], e_s.at[3], e_r.at[3], (o, down)),
    ]
    rims = [
        remote(packed.at[side], edge_q.at[side, o], h_s.at[side, k], h_r.at[side, k], (peer(k), to))
        for k in ORDER + (0,)
        for side, to in enumerate((up, down))
    ]
    for c in edges + rims:
        c.start()
    for f in range(FIELDS):
        picked[o, f] = slot[o, f]

    for c in loads[3:]:
        c.wait()
    col = lax.broadcasted_iota(jnp.int32, (EXT, 128), 0) - HF
    column = lax.rem(t * CW + col + NC, NC)
    blade = lax.shift_right_logical((col + CW) * BLADES, 11)
    group_of = jnp.zeros((EXT, 128), jnp.int32)
    per = BLADES // TILES
    for b in range(per - 1, 2 * per + 1):
        group_of = jnp.where(blade == b, group_s[lax.rem(t * per + b + BLADES - per, BLADES)], group_of)
    for a in range(AMP):
        wave = jnp.broadcast_to(harm_v[:, a : a + 1], (EXT, 128))
        for g in range(GRP_DEV):
            pat[g * AMP + a] = jnp.where(group_of == o * GRP_DEV + g, wave, 0.0)
    weight = 1.0 + 2.0 * column.astype(F32) / NC

    for c in gather:
        c.wait_recv()
    spread = []
    for i in range(STEPS):
        for f in range(FIELDS):
            q[i, o, f] = picked[owner_s[i], f]
        for k in ORDER:
            spread.append(remote(q.at[i, o], q.at[i, o], p2_s.at[i, k], p2_r.at[i, k], (peer(k), t)))
            spread[-1].start()

    for c in edges:
        c.wait_recv()
    sub = lax.broadcasted_iota(jnp.int32, (R, 128), 0)
    lan = lax.broadcasted_iota(jnp.int32, (R, 128), 1)
    for side, (lo, n) in enumerate(((0, HF), (HF, CW), (HF + CW, HF))):
        links = jnp.broadcast_to(link_v[side], (R, 128)).T
        inverse = jnp.sum(jnp.where(links == lan, sub, 0), axis=0, keepdims=True)
        idx[lo : lo + n, :] = jnp.broadcast_to(inverse, (n, 128))
        idx_t[lo : lo + n, :] = jnp.broadcast_to(link_v[side], (n, 128))

    for f in range(FIELDS):
        force = f_ext[f]
        wf[f] = force * weight
        for s in range(SOL):
            mu_a[s, f] = force * pat[s]
            src[s, f] = mu_a[s, f] * UNIT**2
    for lo in (0, HF + CW):
        for f in range(FIELDS):
            for m in range(2):
                dual[m, f, lo : lo + HF, :] = jnp.zeros((HF, R), F32)
            for s in range(SOL):
                mu_b[s, f, lo : lo + HF, :] = jnp.zeros((HF, R), F32)

    def stencil(m2, m1, m0, p1, p2, perm):
        moved = jnp.take_along_axis(m0, perm, axis=1, mode="promise_in_bounds")
        return C0 * m0 + C1 * (m1 + p1) + C2 * (m2 + p2) + moved

    def advance(mu, s, e0, perm, mix):
        near = [[mu[s, f, pl.ds(e0 + k, 8), :] for k in (-2, -1, 0, 1, 2)] for f in range(FIELDS)]
        d = [near[f][3] - near[f][1] for f in range(FIELDS)]
        new = []
        for e in range(FIELDS):
            v = stencil(*near[e], perm)
            for f in range(FIELDS):
                v = v + mix(f, e) * d[f]
            new.append(v)
        return new

    def constant(f, e):
        return flux_s[f, e]

    def mixed(co):
        def mix(f, e):
            if e == 1:
                return co[f]
            return co[FIELDS + DIAG.index(e)] if e == f else flux_s[f, e]

        return mix

    def early(j, carry):
        e0 = 4 + 8 * j
        rows = pl.ds(e0, 8)
        perm = idx[rows, :]
        fs = [f_ext[f, rows, :] * UNIT for f in range(FIELDS)]

        def some(p, carry):
            for r in range(UNROLL):
                s = p * UNROLL + r
                new = advance(mu_a, s, e0, perm, constant)
                ps = pat[s, rows, :]
                for f in range(FIELDS):
                    mu_b[s, f, rows, :] = new[f] + fs[f] * ps
            return carry

        return lax.fori_loop(0, SOL // UNROLL, some, carry)

    lax.fori_loop(0, 17, early, 0)

    def state(n):
        for k in range(1, N_OUT):
            spread[n * (N_OUT - 1) + k - 1].wait_recv()

        def write(rows, half):
            for f in range(FIELDS):
                v = half[f] + flux_s[f, 1]
                coef[n, f, rows, :] = v + half[1] if f == 1 else v
            for m, e in enumerate(DIAG):
                coef[n, FIELDS + m, rows, :] = half[1] + flux_s[e, e]
            if n == STEPS - 1:
                for f in range(FIELDS):
                    halves[f, rows, :] = half[f]

        def body(b, carry):
            write(pl.ds(pl.multiple_of(HF + b * CH, 8), CH), [0.5 * q[n, b, f].astype(F32) for f in range(FIELDS)])
            return carry

        lax.fori_loop(0, N_OUT, body, 0)
        for side, lo in enumerate((HF - HQ, HF + CW)):
            wide[...] = edge_q[side, owner_s[n]].astype(F32)
            write(pl.ds(lo, HQ), [0.5 * wide[HQ * f : HQ * (f + 1), :] for f in range(FIELDS)])

    for c in rims:
        c.wait_recv()

    def turn(n, x):
        def body(j, carry):
            for r in range(PAIR):
                rows = pl.ds(jnp.minimum(HF - HQ + 8 * (j * PAIR + r), HF + CW + HQ - 8), 8)
                mix = mixed([coef[n, m, rows, :] for m in range(9)])
                v = [x[e, rows, :] for e in range(FIELDS)]
                for f in range(FIELDS):
                    w = mix(f, 0) * v[0]
                    for e in range(1, FIELDS):
                        w = w + mix(f, e) * v[e]
                    back[f, rows, :] = w
            return carry

        lax.fori_loop(0, 18 // PAIR, body, 0)

    def adjoint_at(x, f, e0):
        near = [x[f, pl.ds(e0 + k, 8), :] for k in (-2, -1, 0, 1, 2)]
        w = back[f, pl.ds(e0 - 1, 8), :] - back[f, pl.ds(e0 + 1, 8), :]
        return (stencil(*near, idx_t[pl.ds(e0, 8), :]) + w) * (1.0 / UNIT)

    def push(n, x, to):
        state(n)
        turn(n, x)

        def body(j, carry):
            for r in range(PAIR):
                e0 = jnp.minimum(4 + 8 * (j * PAIR + r), HF + CW - 4)
                for f in range(FIELDS):
                    to[f, pl.ds(e0, 8), :] = wf[f, pl.ds(e0, 8), :] + adjoint_at(x, f, e0)
            return carry

        lax.fori_loop(0, 18 // PAIR, body, 0)

    push(0, wf, dual.at[0])
    push(1, dual.at[0], dual.at[1])
    state(2)
    turn(2, dual.at[1])

    def weigh(j, sums):
        for r in range(WIDE):
            e0 = pl.multiple_of(HF + 8 * (j * WIDE + r), 8)
            rows = pl.ds(e0, 8)
            p = None
            for f in range(FIELDS):
                v = dual[0, f, rows, :] + dual[1, f, rows, :] - 2.0 * wf[f, rows, :] + adjoint_at(dual.at[1], f, e0)
                v = v * f_ext[f, rows, :]
                p = v if p is None else p + v
            sums = tuple(sums[s] + p * pat[s, rows, :] for s in range(SOL))
        return sums

    sums = lax.fori_loop(0, CW // 8 // WIDE, weigh, (jnp.zeros((8, 128), F32),) * SOL)

    for s in range(SOL):
        sall[t, s : s + 1, :] = jnp.sum(sums[s], axis=0, keepdims=True)
    terms = []
    for k in range(1, TILES):
        terms.append(remote(sall.at[t], sall.at[t], s_s.at[k], s_r.at[k], (o, lax.rem(t + k, TILES))))
        terms[-1].start()

    def finish(j, carry):
        e0 = 4 + 8 * j
        rows = pl.ds(e0, 8)
        half = [halves[f, rows, :] for f in range(FIELDS)]
        for s in range(SOL):
            d = [mu_a[s, f, pl.ds(e0 + 1, 8), :] - mu_a[s, f, pl.ds(e0 - 1, 8), :] for f in range(FIELDS)]
            dot = half[0] * d[0]
            for f in range(1, FIELDS):
                dot = dot + half[f] * d[f]
            for f in range(FIELDS):
                v = mu_b[s, f, rows, :] + half[1] * d[f]
                mu_b[s, f, rows, :] = v + dot if f == 1 else v
        return carry

    lax.fori_loop(0, 17, finish, 0)

    def second(j, carry):
        e0 = 4 + 8 * j
        rows = pl.ds(e0, 8)
        perm = idx[rows, :]
        mix = mixed([coef[1, m, rows, :] for m in range(9)])

        def some(p, carry):
            for r in range(UNROLL):
                s = p * UNROLL + r
                new = advance(mu_b, s, e0, perm, mix)
                for f in range(FIELDS):
                    mu_a[s, f, rows, :] = new[f] + src[s, f, rows, :]
            return carry

        return lax.fori_loop(0, SOL // UNROLL, some, carry)

    lax.fori_loop(0, 17, second, 0)

    def third(s, carry):
        def some(p, carry):
            for r in range(UNROLL):
                e0 = pl.multiple_of(HF + 8 * (p * UNROLL + r), 8)
                rows = pl.ds(e0, 8)
                new = advance(mu_a, s, e0, idx[rows, :], mixed([coef[0, m, rows, :] for m in range(9)]))
                for f in range(FIELDS):
                    res[s, f, pl.ds(pl.multiple_of(e0 - HF, 8), 8), :] = new[f]
            return carry

        lax.fori_loop(0, CW // 8 // UNROLL, some, 0)
        return carry

    lax.fori_loop(0, SOL, third, 0)

    for c in terms:
        c.wait_recv()
    total = sall[0]
    for k in range(1, TILES):
        total = total + sall[k]
    total = jnp.sum(total, axis=1, keepdims=True) * (1.0 / math.sqrt(FIELDS * R * NC))
    row8 = lax.broadcasted_iota(jnp.int32, (SOL, 128), 0)
    lane8 = lax.broadcasted_iota(jnp.int32, (SOL, 128), 1)
    for g in range(GRP_DEV):
        line = jnp.sum(jnp.where(row8 == lane8 + g * AMP, total, 0.0), axis=0, keepdims=True)
        sens_ref[g : g + 1, :] = line[:, :AMP]

    for c in terms + edges + rims + gather + spread:
        c.wait_send()


def flip(turned_ref, sens_ref, out_hbm, sens_out, res, sem):
    sens_out[...] = sens_ref[...]
    copies = [pltpu.make_async_copy(res.at[s], out_hbm.at[s], sem.at[s]) for s in range(SOL)]
    for s in range(SOL):
        for f in range(FIELDS):
            res[s, f] = (turned_ref[s, f] * UNIT**-STEPS).T
        copies[s].start()
    for c in copies:
        c.wait()


def on_device(checkpoints, owner, flux_matrix, row_link, blade_group, forcing):
    hbm = pl.BlockSpec(memory_space=pltpu.HBM)
    vmem = pl.BlockSpec(memory_space=pltpu.VMEM)
    bf16 = jnp.bfloat16
    dma = pltpu.SemaphoreType.DMA
    shapes = (
        jax.ShapeDtypeStruct((SOL, FIELDS, R, CW), F32),
        jax.ShapeDtypeStruct((GRP_DEV, AMP), F32),
    )
    turned, sens = pl.pallas_call(
        kernel,
        out_shape=shapes,
        in_specs=[hbm] * 7,
        out_specs=(vmem, vmem),
        scratch_shapes=[
            pltpu.SMEM((N_OUT,), jnp.int32),
            pltpu.SMEM((FIELDS, FIELDS), F32),
            pltpu.SMEM((BLADES,), jnp.int32),
            pltpu.VMEM((FIELDS, R, CW), bf16),
            pltpu.VMEM((FIELDS, R, CW), F32),
            pltpu.VMEM((EXT, 128), F32),
            pltpu.VMEM((3, 1, R), jnp.int32),
            pltpu.VMEM((N_OUT, FIELDS, CH, R), bf16),
            pltpu.VMEM((N_OUT, FIELDS, CH, R), bf16),
            pltpu.VMEM((STEPS, N_OUT, FIELDS, CH, R), bf16),
            pltpu.VMEM((2, 32, R), F32),
            pltpu.VMEM((2, 32, R), bf16),
            pltpu.VMEM((2, N_OUT, 32, R), bf16),
            pltpu.VMEM((32, R), F32),
            pltpu.VMEM((FIELDS, EXT, R), F32),
            pltpu.VMEM((EXT, R), jnp.int32),
            pltpu.VMEM((EXT, R), jnp.int32),
            pltpu.VMEM((STEPS, 9, EXT, R), F32),
            pltpu.VMEM((FIELDS, EXT, R), F32),
            pltpu.VMEM((SOL, EXT, R), F32),
            pltpu.VMEM((FIELDS, EXT, R), F32),
            pltpu.VMEM((2, FIELDS, EXT, R), F32),
            pltpu.VMEM((SOL, FIELDS, EXT, R), F32),
            pltpu.VMEM((SOL, FIELDS, EXT, R), F32),
            pltpu.VMEM((SOL, FIELDS, EXT, R), F32),
            pltpu.VMEM((FIELDS, EXT, R), F32),
            pltpu.VMEM((TILES, SOL, 128), F32),
            dma((7,)),
            dma((N_OUT,)),
            dma((N_OUT,)),
            dma((STEPS, N_OUT)),
            dma((STEPS, N_OUT)),
            dma((2, N_OUT)),
            dma((2, N_OUT)),
            dma((4,)),
            dma((4,)),
            dma((TILES,)),
            dma((TILES,)),
        ],
        compiler_params=pltpu.CompilerParams(collective_id=0, has_side_effects=True, vmem_limit_bytes=28 << 20),
    )(
        *(
            pltpu.with_memory_space_constraint(x, pltpu.HBM)
            for x in (owner, flux_matrix, blade_group, jnp.asarray(harmonics()), row_link, checkpoints[0], forcing)
        )
    )
    adjoint, sens = pl.pallas_call(
        flip,
        out_shape=shapes,
        in_specs=[vmem, vmem],
        out_specs=(hbm, vmem),
        scratch_shapes=[pltpu.VMEM((SOL, FIELDS, R, CW), F32), dma((SOL,))],
        compiler_params=pltpu.CompilerParams(vmem_limit_bytes=8 << 20),
    )(turned, sens)
    return adjoint.reshape(GRP_DEV, AMP, FIELDS, R, CW), sens


def solution(mesh):
    return jax.shard_map(
        on_device,
        mesh=mesh,
        in_specs=(P("out", None, None, "blk"), P(), P(), P("blk", None), P(), P(None, None, "blk")),
        out_specs=(P("out", None, None, None, "blk"), P("out", None)),
        check_vma=False,
    )
```

```python
import functools
import math

import jax
import jax.numpy as jnp
import numpy as np
from jax import lax
from jax.experimental import pallas as pl
from jax.experimental.pallas import tpu as pltpu
from jax.sharding import PartitionSpec as P

FIELDS = 5
BLADES = 96
AMP = 4
GRP_DEV = 2
STEPS = 3
R = 128
CW = 128
TILES = 16
NC = TILES * CW
N_OUT = 8
SOL = GRP_DEV * AMP
CH = CW // N_OUT
HQ = 5
HF = 8
EXT = CW + 2 * HF

time_step = 0.25
second_diff = 0.1
fourth_diff = 0.02
link_weight = 0.5

UNIT = 1.0 / (time_step * link_weight)
C0 = UNIT * (1.0 - time_step * (2.0 * second_diff + 6.0 * fourth_diff + link_weight))
C1 = UNIT * time_step * (second_diff + 4.0 * fourth_diff)
C2 = -UNIT * time_step * fourth_diff

MESH = pl.DeviceIdType.MESH
F32 = jnp.float32
DIAG = (0, 2, 3, 4)
UNROLL = 8
ORDER = (5, 3, 7, 4, 1, 2, 6)
PAIR = 6
WIDE = 8


def harmonics():
    c = np.arange(-HF, CW + HF)
    phase = ((c * BLADES) % NC) / NC
    rows = [
        (np.cos if a % 2 == 0 else np.sin)(2.0 * math.pi * (a // 2 + 1) * phase) for a in range(AMP)
    ]
    table = np.zeros((EXT, 128), np.float32)
    table[:, :AMP] = np.stack(rows, axis=1)
    return table


def kernel(
    owner_hbm, flux_hbm, group_hbm, harm_hbm, link_hbm, ckpt_hbm, force_hbm,
    res, sens_ref,
    owner_s, flux_s, group_s, ckpt_v, force_v, harm_v, link_v, slot, picked, q, pack, packed, edge_q, wide, f_ext, idx, idx_t, coef, halves, pat, wf, dual,
    mu_a, mu_b, src, back, sall,
    in_sem, p1_s, p1_r, p2_s, p2_r, h_s, h_r, e_s, e_r, s_s, s_r,
):
    o = lax.axis_index("out")
    t = lax.axis_index("blk")
    up = lax.rem(t + 1, TILES)

    def peer(k):
        return lax.rem(o // 2 + k // 2, N_OUT // 2) * 2 + lax.rem(o + k, 2)

    down = lax.rem(t + TILES - 1, TILES)

    loads = [
        pltpu.make_async_copy(src, dst, in_sem.at[i])
        for i, (src, dst) in enumerate(
            ((ckpt_hbm, ckpt_v), (force_hbm, force_v), (link_hbm, link_v.at[1]), (harm_hbm, harm_v),
             (group_hbm, group_s), (owner_hbm, owner_s), (flux_hbm, flux_s))
        )
    ]
    for c in loads:
        c.start()

    barrier = pltpu.get_barrier_semaphore()
    count = 0
    for k in ORDER:
        pl.semaphore_signal(barrier, inc=1, device_id=(peer(k), t), device_id_type=MESH)
        count += 1
    for side in (up, down):
        for k in ORDER + (0,):
            pl.semaphore_signal(barrier, inc=1, device_id=(peer(k), side), device_id_type=MESH)
            count += 1
    for k in range(2, TILES - 1):
        pl.semaphore_signal(barrier, inc=1, device_id=(o, lax.rem(t + k, TILES)), device_id_type=MESH)
        count += 1

    def remote(src, dst, send, recv, device):
        return pltpu.make_async_remote_copy(
            src_ref=src, dst_ref=dst, send_sem=send, recv_sem=recv, device_id=device, device_id_type=MESH
        )

    pack[...] = jnp.zeros_like(pack)
    loads[0].wait()
    for f in range(FIELDS):
        turned = ckpt_v[f].astype(F32).T
        for b in range(N_OUT):
            slot[b, f] = turned[b * CH : (b + 1) * CH].astype(jnp.bfloat16)
        pack[0, HQ * f : HQ * (f + 1), :] = turned[CW - HQ :]
        pack[1, HQ * f : HQ * (f + 1), :] = turned[:HQ]
    packed[...] = pack[...].astype(jnp.bfloat16)

    pl.semaphore_wait(barrier, count)

    gather = []
    for k in ORDER:
        to = peer(k)
        gather.append(remote(slot.at[to], picked.at[o], p1_s.at[k], p1_r.at[k], (to, t)))
        gather[-1].start()
    loads[1].wait()
    for f in range(FIELDS):
        f_ext[f, HF : HF + CW, :] = force_v[f].T
    loads[2].wait()
    edges = [
        remote(f_ext.at[:, pl.ds(CW, HF), :], f_ext.at[:, pl.ds(0, HF), :], e_s.at[0], e_r.at[0], (o, up)),
        remote(f_ext.at[:, pl.ds(HF, HF), :], f_ext.at[:, pl.ds(HF + CW, HF), :], e_s.at[1], e_r.at[1], (o, down)),
        remote(link_v.at[1], link_v.at[0], e_s.at[2], e_r.at[2], (o, up)),
        remote(link_v.at[1], link_v.at[2], e_s.at[3], e_r.at[3], (o, down)),
    ]
    rims = [
        remote(packed.at[side], edge_q.at[side, o], h_s.at[side, k], h_r.at[side, k], (peer(k), to))
        for k in ORDER + (0,)
        for side, to in enumerate((up, down))
    ]
    for c in edges + rims:
        c.start()
    for f in range(FIELDS):
        picked[o, f] = slot[o, f]

    for c in loads[3:]:
        c.wait()
    col = lax.broadcasted_iota(jnp.int32, (EXT, 128), 0) - HF
    column = lax.rem(t * CW + col + NC, NC)
    blade = lax.shift_right_logical((col + CW) * BLADES, 11)
    group_of = jnp.zeros((EXT, 128), jnp.int32)
    per = BLADES // TILES
    for b in range(per - 1, 2 * per + 1):
        group_of = jnp.where(blade == b, group_s[lax.rem(t * per + b + BLADES - per, BLADES)], group_of)
    for a in range(AMP):
        wave = jnp.broadcast_to(harm_v[:, a : a + 1], (EXT, 128))
        for g in range(GRP_DEV):
            pat[g * AMP + a] = jnp.where(group_of == o * GRP_DEV + g, wave, 0.0)
    weight = 1.0 + 2.0 * column.astype(F32) / NC

    for c in gather:
        c.wait_recv()
    spread = []
    for i in range(STEPS):
        for f in range(FIELDS):
            q[i, o, f] = picked[owner_s[i], f]
        for k in ORDER:
            spread.append(remote(q.at[i, o], q.at[i, o], p2_s.at[i, k], p2_r.at[i, k], (peer(k), t)))
            spread[-1].start()

    for c in edges:
        c.wait_recv()
    sub = lax.broadcasted_iota(jnp.int32, (R, 128), 0)
    lan = lax.broadcasted_iota(jnp.int32, (R, 128), 1)
    for side, (lo, n) in enumerate(((0, HF), (HF, CW), (HF + CW, HF))):
        links = jnp.broadcast_to(link_v[side], (R, 128)).T
        inverse = jnp.sum(jnp.where(links == lan, sub, 0), axis=0, keepdims=True)
        idx[lo : lo + n, :] = jnp.broadcast_to(inverse, (n, 128))
        idx_t[lo : lo + n, :] = jnp.broadcast_to(link_v[side], (n, 128))

    for f in range(FIELDS):
        force = f_ext[f]
        wf[f] = force * weight
        for s in range(SOL):
            mu_a[s, f] = force * pat[s]
            src[s, f] = mu_a[s, f] * UNIT**2
    for lo in (0, HF + CW):
        for f in range(FIELDS):
            for m in range(2):
                dual[m, f, lo : lo + HF, :] = jnp.zeros((HF, R), F32)
            for s in range(SOL):
                mu_b[s, f, lo : lo + HF, :] = jnp.zeros((HF, R), F32)

    def stencil(m2, m1, m0, p1, p2, perm):
        moved = jnp.take_along_axis(m0, perm, axis=1, mode="promise_in_bounds")
        return C0 * m0 + C1 * (m1 + p1) + C2 * (m2 + p2) + moved

    def advance(mu, s, e0, perm, mix):
        near = [[mu[s, f, pl.ds(e0 + k, 8), :] for k in (-2, -1, 0, 1, 2)] for f in range(FIELDS)]
        d = [near[f][3] - near[f][1] for f in range(FIELDS)]
        new = []
        for e in range(FIELDS):
            v = stencil(*near[e], perm)
            for f in range(FIELDS):
                v = v + mix(f, e) * d[f]
            new.append(v)
        return new

    def constant(f, e):
        return flux_s[f, e]

    def mixed(co):
        def mix(f, e):
            if e == 1:
                return co[f]
            return co[FIELDS + DIAG.index(e)] if e == f else flux_s[f, e]

        return mix

    def early(j, carry):
        e0 = 4 + 8 * j
        rows = pl.ds(e0, 8)
        perm = idx[rows, :]
        fs = [f_ext[f, rows, :] * UNIT for f in range(FIELDS)]

        def some(p, carry):
            for r in range(UNROLL):
                s = p * UNROLL + r
                new = advance(mu_a, s, e0, perm, constant)
                ps = pat[s, rows, :]
                for f in range(FIELDS):
                    mu_b[s, f, rows, :] = new[f] + fs[f] * ps
            return carry

        return lax.fori_loop(0, SOL // UNROLL, some, carry)

    lax.fori_loop(0, 17, early, 0)

    def state(n):
        for k in range(1, N_OUT):
            spread[n * (N_OUT - 1) + k - 1].wait_recv()

        def write(rows, half):
            for f in range(FIELDS):
                v = half[f] + flux_s[f, 1]
                coef[n, f, rows, :] = v + half[1] if f == 1 else v
            for m, e in enumerate(DIAG):
                coef[n, FIELDS + m, rows, :] = half[1] + flux_s[e, e]
            if n == STEPS - 1:
                for f in range(FIELDS):
                    halves[f, rows, :] = half[f]

        def body(b, carry):
            write(pl.ds(pl.multiple_of(HF + b * CH, 8), CH), [0.5 * q[n, b, f].astype(F32) for f in range(FIELDS)])
            return carry

        lax.fori_loop(0, N_OUT, body, 0)
        for side, lo in enumerate((HF - HQ, HF + CW)):
            wide[...] = edge_q[side, owner_s[n]].astype(F32)
            write(pl.ds(lo, HQ), [0.5 * wide[HQ * f : HQ * (f + 1), :] for f in range(FIELDS)])

    for c in rims:
        c.wait_recv()

    def turn(n, x):
        def body(j, carry):
            for r in range(PAIR):
                rows = pl.ds(jnp.minimum(HF - HQ + 8 * (j * PAIR + r), HF + CW + HQ - 8), 8)
                mix = mixed([coef[n, m, rows, :] for m in range(9)])
                v = [x[e, rows, :] for e in range(FIELDS)]
                for f in range(FIELDS):
                    w = mix(f, 0) * v[0]
                    for e in range(1, FIELDS):
                        w = w + mix(f, e) * v[e]
                    back[f, rows, :] = w
            return carry

        lax.fori_loop(0, 18 // PAIR, body, 0)

    def adjoint_at(x, f, e0):
        near = [x[f, pl.ds(e0 + k, 8), :] for k in (-2, -1, 0, 1, 2)]
        w = back[f, pl.ds(e0 - 1, 8), :] - back[f, pl.ds(e0 + 1, 8), :]
        return (stencil(*near, idx_t[pl.ds(e0, 8), :]) + w) * (1.0 / UNIT)

    def push(n, x, to):
        state(n)
        turn(n, x)

        def body(j, carry):
            for r in range(PAIR):
                e0 = jnp.minimum(4 + 8 * (j * PAIR + r), HF + CW - 4)
                for f in range(FIELDS):
                    to[f, pl.ds(e0, 8), :] = wf[f, pl.ds(e0, 8), :] + adjoint_at(x, f, e0)
            return carry

        lax.fori_loop(0, 18 // PAIR, body, 0)

    push(0, wf, dual.at[0])
    push(1, dual.at[0], dual.at[1])
    state(2)
    turn(2, dual.at[1])

    def weigh(j, sums):
        for r in range(WIDE):
            e0 = pl.multiple_of(HF + 8 * (j * WIDE + r), 8)
            rows = pl.ds(e0, 8)
            p = None
            for f in range(FIELDS):
                v = dual[0, f, rows, :] + dual[1, f, rows, :] - 2.0 * wf[f, rows, :] + adjoint_at(dual.at[1], f, e0)
                v = v * f_ext[f, rows, :]
                p = v if p is None else p + v
            sums = tuple(sums[s] + p * pat[s, rows, :] for s in range(SOL))
        return sums

    sums = lax.fori_loop(0, CW // 8 // WIDE, weigh, (jnp.zeros((8, 128), F32),) * SOL)

    for s in range(SOL):
        sall[t, s : s + 1, :] = jnp.sum(sums[s], axis=0, keepdims=True)
    terms = []
    for k in range(1, TILES):
        terms.append(remote(sall.at[t], sall.at[t], s_s.at[k], s_r.at[k], (o, lax.rem(t + k, TILES))))
        terms[-1].start()

    def finish(j, carry):
        e0 = 4 + 8 * j
        rows = pl.ds(e0, 8)
        half = [halves[f, rows, :] for f in range(FIELDS)]
        for s in range(SOL):
            d = [mu_a[s, f, pl.ds(e0 + 1, 8), :] - mu_a[s, f, pl.ds(e0 - 1, 8), :] for f in range(FIELDS)]
            dot = half[0] * d[0]
            for f in range(1, FIELDS):
                dot = dot + half[f] * d[f]
            for f in range(FIELDS):
                v = mu_b[s, f, rows, :] + half[1] * d[f]
                mu_b[s, f, rows, :] = v + dot if f == 1 else v
        return carry

    lax.fori_loop(0, 17, finish, 0)

    def second(j, carry):
        e0 = 4 + 8 * j
        rows = pl.ds(e0, 8)
        perm = idx[rows, :]
        mix = mixed([coef[1, m, rows, :] for m in range(9)])

        def some(p, carry):
            for r in range(UNROLL):
                s = p * UNROLL + r
                new = advance(mu_b, s, e0, perm, mix)
                for f in range(FIELDS):
                    mu_a[s, f, rows, :] = new[f] + src[s, f, rows, :]
            return carry

        return lax.fori_loop(0, SOL // UNROLL, some, carry)

    lax.fori_loop(0, 17, second, 0)

    def third(s, carry):
        def some(p, carry):
            for r in range(UNROLL):
                e0 = pl.multiple_of(HF + 8 * (p * UNROLL + r), 8)
                rows = pl.ds(e0, 8)
                new = advance(mu_a, s, e0, idx[rows, :], mixed([coef[0, m, rows, :] for m in range(9)]))
                for f in range(FIELDS):
                    res[s, f, pl.ds(pl.multiple_of(e0 - HF, 8), 8), :] = new[f]
            return carry

        lax.fori_loop(0, CW // 8 // UNROLL, some, 0)
        return carry

    lax.fori_loop(0, SOL, third, 0)

    for c in terms:
        c.wait_recv()
    total = sall[0]
    for k in range(1, TILES):
        total = total + sall[k]
    total = jnp.sum(total, axis=1, keepdims=True) * (1.0 / math.sqrt(FIELDS * R * NC))
    row8 = lax.broadcasted_iota(jnp.int32, (SOL, 128), 0)
    lane8 = lax.broadcasted_iota(jnp.int32, (SOL, 128), 1)
    for g in range(GRP_DEV):
        line = jnp.sum(jnp.where(row8 == lane8 + g * AMP, total, 0.0), axis=0, keepdims=True)
        sens_ref[g : g + 1, :] = line[:, :AMP]

    for c in terms + edges + rims + gather + spread:
        c.wait_send()


def flip(turned_ref, sens_ref, out_hbm, sens_out, res, sem):
    sens_out[...] = sens_ref[...]
    copies = [pltpu.make_async_copy(res.at[s], out_hbm.at[s], sem.at[s]) for s in range(SOL)]
    for s in range(SOL):
        for f in range(FIELDS):
            res[s, f] = (turned_ref[s, f] * UNIT**-STEPS).T
        copies[s].start()
    for c in copies:
        c.wait()


def on_device(checkpoints, owner, flux_matrix, row_link, blade_group, forcing):
    hbm = pl.BlockSpec(memory_space=pltpu.HBM)
    vmem = pl.BlockSpec(memory_space=pltpu.VMEM)
    bf16 = jnp.bfloat16
    dma = pltpu.SemaphoreType.DMA
    shapes = (
        jax.ShapeDtypeStruct((SOL, FIELDS, R, CW), F32),
        jax.ShapeDtypeStruct((GRP_DEV, AMP), F32),
    )
    turned, sens = pl.pallas_call(
        kernel,
        out_shape=shapes,
        in_specs=[hbm] * 7,
        out_specs=(vmem, vmem),
        scratch_shapes=[
            pltpu.SMEM((N_OUT,), jnp.int32),
            pltpu.SMEM((FIELDS, FIELDS), F32),
            pltpu.SMEM((BLADES,), jnp.int32),
            pltpu.VMEM((FIELDS, R, CW), bf16),
            pltpu.VMEM((FIELDS, R, CW), F32),
            pltpu.VMEM((EXT, 128), F32),
            pltpu.VMEM((3, 1, R), jnp.int32),
            pltpu.VMEM((N_OUT, FIELDS, CH, R), bf16),
            pltpu.VMEM((N_OUT, FIELDS, CH, R), bf16),
            pltpu.VMEM((STEPS, N_OUT, FIELDS, CH, R), bf16),
            pltpu.VMEM((2, 32, R), F32),
            pltpu.VMEM((2, 32, R), bf16),
            pltpu.VMEM((2, N_OUT, 32, R), bf16),
            pltpu.VMEM((32, R), F32),
            pltpu.VMEM((FIELDS, EXT, R), F32),
            pltpu.VMEM((EXT, R), jnp.int32),
            pltpu.VMEM((EXT, R), jnp.int32),
            pltpu.VMEM((STEPS, 9, EXT, R), F32),
            pltpu.VMEM((FIELDS, EXT, R), F32),
            pltpu.VMEM((SOL, EXT, R), F32),
            pltpu.VMEM((FIELDS, EXT, R), F32),
            pltpu.VMEM((2, FIELDS, EXT, R), F32),
            pltpu.VMEM((SOL, FIELDS, EXT, R), F32),
            pltpu.VMEM((SOL, FIELDS, EXT, R), F32),
            pltpu.VMEM((SOL, FIELDS, EXT, R), F32),
            pltpu.VMEM((FIELDS, EXT, R), F32),
            pltpu.VMEM((TILES, SOL, 128), F32),
            dma((7,)),
            dma((N_OUT,)),
            dma((N_OUT,)),
            dma((STEPS, N_OUT)),
            dma((STEPS, N_OUT)),
            dma((2, N_OUT)),
            dma((2, N_OUT)),
            dma((4,)),
            dma((4,)),
            dma((TILES,)),
            dma((TILES,)),
        ],
        compiler_params=pltpu.CompilerParams(collective_id=0, has_side_effects=True, vmem_limit_bytes=28 << 20),
    )(
        *(
            pltpu.with_memory_space_constraint(x, pltpu.HBM)
            for x in (owner, flux_matrix, blade_group, jnp.asarray(harmonics()), row_link, checkpoints[0], forcing)
        )
    )
    adjoint, sens = pl.pallas_call(
        flip,
        out_shape=shapes,
        in_specs=[vmem, vmem],
        out_specs=(hbm, vmem),
        scratch_shapes=[pltpu.VMEM((SOL, FIELDS, R, CW), F32), dma((SOL,))],
        compiler_params=pltpu.CompilerParams(vmem_limit_bytes=8 << 20),
    )(turned, sens)
    return adjoint.reshape(GRP_DEV, AMP, FIELDS, R, CW), sens


def solution(mesh):
    return jax.shard_map(
        on_device,
        mesh=mesh,
        in_specs=(P("out", None, None, "blk"), P(), P(), P("blk", None), P(), P(None, None, "blk")),
        out_specs=(P("out", None, None, None, "blk"), P("out", None)),
        check_vma=False,
    )
```
